256 devices in a mesh: pipe: 2 (over y_hi), seq: 32 (over z, y_lo, core), tensor: 4 (over x).
Axes of the slice: x: 4, y: 4 (y_hi: 2, y_lo: 2; y = y_hi * 2 + y_lo), z: 8, core: 2. Of those that a mesh axis runs over, the one named last changes fastest.
Arguments:
- resid: bfloat16 [2, 2, 8192, 8192], P('pipe', None, 'seq', 'tensor'), may hold values from -16 to 16
- streams: bfloat16 [2, 2, 8192, 3, 8192], P('pipe', None, 'seq', None, 'tensor'), may hold values from -6 to 6
- filt: bfloat16 [7, 8192], P(None, 'tensor'), may hold values from -2 to 2
- q_gain: float32 [4096], P('tensor'), may hold values from 0.5 to 2
- k_gain: float32 [4096], P('tensor'), may hold values from 0.1 to 1.9
- out_weight: bfloat16 [4096, 8192], P('seq', 'tensor'), may hold values from -0.09375 to 0.09375
- contig_lengths: int32 [2, 32], replicated, may hold values from 1 to 1024, 8192 in all within a row
Outputs:
- activations: bfloat16 [2, 2, 8192, 8192], P('pipe', None, 'seq', 'tensor')
The draws below stay inside these ranges and needn't reach their ends.
Inputs may be any that keep to these rules, and one draw needn't show every extreme that they name: `contig_lengths`: each micro-batch's contigs lie end to end in order and fill its 8192 tokens; in every micro-batch the longest is exactly 1024 tokens.
All inputs are finite; a program needn't handle non-finite values.
Results may differ from the reference program's by a relative error of at most 0.0062.
Values may be sent and summed in bfloat16 or wider, within the bound.
No kernel may reach another device: no remote copies, remote signals or barrier semaphores. Data moves between devices by JAX's collectives and lax.ppermute only.
A program may use at most 128 MiB of HBM per device.

```python
import math
import jax
import jax.numpy as jnp
import numpy as np
from jax import lax

D = 8192
HD = 128
H = 32
K = 7
MB = 2
TOK_DEV = 256
SPAN = 4
MOST = 1024
L = 8192
NCONTIG = 32
N_PIPE = 2
N_SEQ = 32


def draw_resid(key, part):
    base_key = jax.random.fold_in(key, 0)
    base = jax.random.normal(base_key, (N_PIPE, MB, L, D), jnp.float32)
    return jnp.clip(base, -16.0, 16.0).astype(jnp.bfloat16)


def block_levels(stream_key, shape, cuts, smallest, top_value):
    level = 1.0
    for position, parts in cuts:
        heights = jax.random.uniform(jax.random.fold_in(jax.random.fold_in(stream_key, 6), position), (parts,), jnp.float32, smallest / len(cuts), top_value / len(cuts))
        level = level * jnp.repeat(jnp.exp(heights), shape[position] // parts).reshape((-1,) + (1,) * (len(shape) - 1 - position))
    return level


def profile(number_of, total, most, slope):
    portions = [(1 << 20) // math.isqrt(standing ** slope) + 1 for standing in range(2, number_of + 1)]
    rest, holding = total - most - (number_of - 1), [1] * (number_of - 1)
    while rest > 0:
        free = [i for i in range(number_of - 1) if holding[i] < most]
        mass, budget = sum([portions[i] for i in free]), rest
        for i in free:
            more = min(most - holding[i], max(1, budget * portions[i] // mass), rest)
            holding[i] = holding[i] + more
            rest = rest - more
    return np.array([most] + holding)


def uneven_parts(rng, count, total, most, lean):
    if count == 2:
        one = jax.random.randint(rng, (), max(1, total - most), min(most, total - 1) + 1)
        return jnp.stack([one, total - one])
    sizes = jnp.asarray(profile(count, total, most, lean), jnp.int32)
    pairs = (count - 1) // 2
    giver, receiver = sizes[1:1 + 2 * pairs:2], sizes[2:2 + 2 * pairs:2]
    margin = jnp.minimum(giver - 1, most - receiver)
    shifted = jax.random.randint(jax.random.fold_in(rng, 1), (pairs,), 0, 1 << 20) % (margin + 1)
    sizes = sizes.at[1:1 + 2 * pairs:2].set(giver - shifted).at[2:2 + 2 * pairs:2].set(receiver + shifted)
    return sizes[jax.random.permutation(jax.random.fold_in(rng, 2), count)]


def normal_values(rng, shape, scale, limit, shards=(), held_as=jnp.bfloat16):
    values = scale * jax.random.normal(rng, shape, jnp.float32)
    if shards:
        values = values * block_levels(rng, shape, shards, -0.22, 0.18)
    return jnp.clip(values, -limit, limit).astype(held_as)


def setup_inputs(seed: int = 0) -> dict:
    arg_keys = jax.random.split(jax.random.key(seed), 8)
    resid = draw_resid(jax.random.fold_in(arg_keys[7], 71), 0)
    streams = normal_values(arg_keys[1], (N_PIPE, MB, L, 3, D), 1.0, 6.0, ((0, 2), (2, 32), (4, 4)))
    filt = normal_values(arg_keys[2], (K, D), K ** -0.5, 2.0, ((1, 4),))
    q_gain = jnp.clip(jnp.exp(math.log(2.0) - 1.3862944 * jax.random.uniform(arg_keys[3], (H * HD,), jnp.float32) ** block_levels(arg_keys[3], (H * HD,), ((0, 4),), -0.2, 0.2)), 0.5, 2.0)
    k_gain = jnp.clip(1.0 + 0.18 * jax.random.normal(arg_keys[4], (H * HD,), jnp.float32), 0.1, 1.9)
    out_weight = normal_values(arg_keys[5], (H * HD, D), (H * HD) ** -0.5, 0.09375, ((0, 32), (1, 4)))
    contig_lengths = jax.vmap(lambda own: uneven_parts(own, NCONTIG, L, MOST, 2))(jax.random.split(arg_keys[6], MB)).reshape((MB, NCONTIG)).astype(jnp.int32)
    return {"resid": resid, "streams": streams, "filt": filt, "q_gain": q_gain, "k_gain": k_gain, "out_weight": out_weight, "contig_lengths": contig_lengths}


NEG_FILL = -1e30


def rounded(values):
    return lax.optimization_barrier(values.astype(jnp.bfloat16))


def segment_of(contig_ends, positions):
    return jnp.sum((contig_ends[:, None, :] <= positions[None, :, None]).astype(jnp.int32), axis=2)


def reference(resid, streams, filt, q_gain, k_gain, out_weight, contig_lengths):
    resid_own = resid[0]
    streams_own = streams[0]
    gated = rounded(streams_own[:, :, 0].astype(jnp.float32) * streams_own[:, :, 2].astype(jnp.float32))
    padded = jnp.pad(gated.astype(jnp.float32), ((0, 0), (K - 1, 0), (0, 0)))
    conv_out = jnp.zeros(resid_own.shape, jnp.float32)
    for offset in range(K):
        conv_out = conv_out + filt[offset].astype(jnp.float32) * padded[:, K - 1 - offset:K - 1 - offset + L]
    hidden = rounded(resid_own.astype(jnp.float32) + streams_own[:, :, 1].astype(jnp.float32) * conv_out)
    attend = hidden.reshape(MB, L, H, 2, HD)[:, :, :, 0].reshape(MB, L, H * HD)
    contig_ends = jnp.cumsum(contig_lengths, axis=1).astype(jnp.int32)
    window = SPAN * TOK_DEV
    queries = rounded(attend.astype(jnp.float32) * q_gain)
    keys = rounded(attend.astype(jnp.float32) * k_gain)
    keys_pad = jnp.pad(keys, ((0, 0), (window, 0), (0, 0)))
    values_pad = jnp.pad(attend, ((0, 0), (window, 0), (0, 0)))

    def one_block(index):
        start = (index * TOK_DEV).astype(jnp.int32)
        query_pos = start + jnp.arange(TOK_DEV, dtype=jnp.int32)
        key_pos = start - window + jnp.arange(window + TOK_DEV, dtype=jnp.int32)
        q_block = lax.dynamic_slice_in_dim(queries, start, TOK_DEV, 1).astype(jnp.float32).reshape(MB, TOK_DEV, H, HD)
        k_block = lax.dynamic_slice_in_dim(keys_pad, start, window + TOK_DEV, 1).astype(jnp.float32).reshape(MB, window + TOK_DEV, H, HD)
        v_block = lax.dynamic_slice_in_dim(values_pad, start, window + TOK_DEV, 1).astype(jnp.float32).reshape(MB, window + TOK_DEV, H, HD)
        same = segment_of(contig_ends, query_pos)[:, :, None] == segment_of(contig_ends, key_pos)[:, None, :]
        causal = (key_pos[None, None, :] <= query_pos[None, :, None]) & (key_pos[None, None, :] >= 0)
        visible = (same & causal)[:, None]
        scores = jnp.einsum('mthd,mshd->mhts', q_block, k_block) / HD
        scores = jnp.where(visible, scores, NEG_FILL)
        top = jnp.max(scores, axis=-1, keepdims=True)
        weights = jnp.where(visible, jnp.exp(scores - top), 0.0)
        total = jnp.sum(weights, axis=-1)
        mixed = jnp.einsum('mhts,mshd->mthd', rounded(weights).astype(jnp.float32), v_block)
        mixed = mixed / jnp.transpose(total, (0, 2, 1))[..., None]
        return mixed.astype(jnp.bfloat16).reshape(MB, TOK_DEV, H * HD)

    blocks = lax.map(one_block, jnp.arange(N_SEQ, dtype=jnp.int32))
    mixed = jnp.transpose(blocks, (1, 0, 2, 3)).reshape(MB * L, H * HD)
    projected = jnp.dot(mixed, out_weight, preferred_element_type=jnp.float32)
    projected = projected.astype(jnp.bfloat16).reshape(MB, L, D)
    return jnp.stack([hidden, projected])
```

```python
import jax
import jax.numpy as jnp
from jax import lax
from jax.experimental import pallas as pl
from jax.experimental.pallas import tpu as pltpu
from jax.sharding import PartitionSpec as P

HD = 128
NEG_FILL = -1e30
HALO = 8
COLS = 512
ROWS = 32


def shifted(value, axis, pairs):
    return lax.ppermute(value, axis, pairs)


def tail_body(stream, tail):
    for b in range(stream.shape[0]):
        gate = stream[b, 0].astype(jnp.float32) * stream[b, 2].astype(jnp.float32)
        tail[b] = gate.astype(jnp.bfloat16)


def tail_of(streams):
    batches, kinds, rows, width = streams.shape
    return pl.pallas_call(
        tail_body,
        grid=(1,),
        in_specs=[pl.BlockSpec((batches, kinds, HALO, width), lambda i: (0, 0, rows // HALO - 1, 0))],
        out_specs=pl.BlockSpec((batches, HALO, width), lambda i: (0, 0, 0)),
        out_shape=jax.ShapeDtypeStruct((batches, HALO, width), jnp.bfloat16),
        name="tail",
    )(streams)


def hyena_body(stream, resid, prev, filt, hidden, attend, extended):
    taps = filt.shape[0]
    rows, cols = resid.shape
    extended[0:HALO] = prev[...].astype(jnp.float32)
    for r in range(0, rows, ROWS):
        gate = stream[0, r : r + ROWS].astype(jnp.float32) * stream[2, r : r + ROWS].astype(jnp.float32)
        extended[HALO + r : HALO + r + ROWS] = gate.astype(jnp.bfloat16).astype(jnp.float32)
    weights = [filt[j : j + 1].astype(jnp.float32) for j in range(taps)]
    for r in range(0, rows, ROWS):
        conv = weights[0] * extended[HALO + r : HALO + r + ROWS]
        for j in range(1, taps):
            conv = conv + weights[j] * extended[HALO + r - j : HALO + r - j + ROWS]
        mixed = resid[r : r + ROWS].astype(jnp.float32) + stream[1, r : r + ROWS].astype(jnp.float32) * conv
        mixed = mixed.astype(jnp.bfloat16)
        hidden[r : r + ROWS] = mixed
        for c in range(cols // (2 * HD)):
            attend[r : r + ROWS, c * HD : (c + 1) * HD] = mixed[:, 2 * c * HD : (2 * c + 1) * HD]


def hyena(streams, resid, prev, filt, batch):
    _, _, rows, width = streams.shape
    taps = filt.shape[0]
    return pl.pallas_call(
        hyena_body,
        grid=(width // COLS,),
        in_specs=[
            pl.BlockSpec((None, 3, rows, COLS), lambda c: (batch, 0, 0, c)),
            pl.BlockSpec((None, rows, COLS), lambda c: (batch, 0, c)),
            pl.BlockSpec((None, HALO, COLS), lambda c: (batch, 0, c)),
            pl.BlockSpec((taps, COLS), lambda c: (0, c)),
        ],
        out_specs=[
            pl.BlockSpec((rows, COLS), lambda c: (0, c)),
            pl.BlockSpec((rows, COLS // 2), lambda c: (0, c)),
        ],
        out_shape=[
            jax.ShapeDtypeStruct((rows, width), jnp.bfloat16),
            jax.ShapeDtypeStruct((rows, width // 2), jnp.bfloat16),
        ],
        scratch_shapes=[pltpu.VMEM((HALO + rows, COLS), jnp.float32)],
        cost_estimate=pl.CostEstimate(flops=20 * rows * width, bytes_accessed=11 * rows * width, transcendentals=0),
        name="hyena",
    )(streams, resid, prev, filt)


def attention_body(meta, own, p1, p2, p3, p4, low, q_gain, k_gain, mixed, acc, top, total):
    rows = own.shape[0]
    query = (own[...].astype(jnp.float32) * q_gain[...]).astype(jnp.bfloat16)
    lowest = low[:, 0:1]
    row = lax.broadcasted_iota(jnp.int32, (rows, rows), 0)
    col = lax.broadcasted_iota(jnp.int32, (rows, rows), 1)

    def scores_of(piece):
        key = (piece.astype(jnp.float32) * k_gain[...]).astype(jnp.bfloat16)
        return lax.dot_general(
            query, key, (((1,), (1,)), ((), ())), preferred_element_type=jnp.float32
        ) * (1.0 / HD)

    def weighted(weights, piece):
        return jnp.dot(weights.astype(jnp.bfloat16), piece, preferred_element_type=jnp.float32)

    value = own[...]
    scores = scores_of(value)
    scores = jnp.where((col + meta[0] >= lowest) & (col <= row), scores, NEG_FILL)
    best = jnp.max(scores, axis=1, keepdims=True)
    weights = jnp.exp(scores - best)
    top[...] = best
    total[...] = jnp.sum(weights, axis=1, keepdims=True)
    acc[...] = weighted(weights, value)
    for k, ref in enumerate((p1, p2, p3, p4), 1):

        @pl.when(meta[8 + k] > 0)
        def _(k=k, ref=ref):
            piece = ref[...]
            part = jnp.where(col + meta[k] >= lowest, scores_of(piece), NEG_FILL)
            old = top[...]
            new = jnp.maximum(old, jnp.max(part, axis=1, keepdims=True))
            scale = jnp.exp(old - new)
            part = jnp.exp(part - new)
            top[...] = new
            total[...] = total[...] * scale + jnp.sum(part, axis=1, keepdims=True)
            acc[...] = acc[...] * scale + weighted(part, piece)

    mixed[...] = (acc[...] / total[...]).astype(jnp.bfloat16)


def attention(meta, pieces, low, q_gain, k_gain):
    rows, width = pieces[0].shape
    heads = width // HD
    by_head = pl.BlockSpec((rows, HD), lambda g, meta: (0, g))
    gain = pl.BlockSpec((1, HD), lambda g, meta: (0, g))
    return pl.pallas_call(
        attention_body,
        grid_spec=pltpu.PrefetchScalarGridSpec(
            num_scalar_prefetch=1,
            grid=(heads,),
            in_specs=[by_head] * 5 + [pl.BlockSpec((rows, HD), lambda g, meta: (0, 0)), gain, gain],
            out_specs=by_head,
            scratch_shapes=[
                pltpu.VMEM((rows, HD), jnp.float32),
                pltpu.VMEM((rows, 1), jnp.float32),
                pltpu.VMEM((rows, 1), jnp.float32),
            ],
        ),
        out_shape=jax.ShapeDtypeStruct((rows, width), jnp.bfloat16),
        cost_estimate=pl.CostEstimate(
            flops=4 * 5 * rows * rows * width, bytes_accessed=12 * rows * width, transcendentals=5 * rows * rows * heads
        ),
        name="attention",
    )(meta, *pieces, low, q_gain, k_gain)


def project_body(order, a0, a1, a2, a3, w0, w1, w2, w3, out):
    total = jnp.dot(a0[...], w0[...], preferred_element_type=jnp.float32)
    for a, w in ((a1, w1), (a2, w2), (a3, w3)):
        total = total + jnp.dot(a[...], w[...], preferred_element_type=jnp.float32)
    out[...] = total.astype(jnp.bfloat16)


def project(order, parts, weight, block=256):
    rows, depth = parts[0].shape
    width = weight.shape[1]

    def w_spec(k):
        return pl.BlockSpec((depth, block), lambda n, order: (order[k], n))

    return pl.pallas_call(
        project_body,
        grid_spec=pltpu.PrefetchScalarGridSpec(
            num_scalar_prefetch=1,
            grid=(width // block,),
            in_specs=[pl.BlockSpec((rows, depth), lambda n, order: (0, 0))] * 4 + [w_spec(k) for k in range(4)],
            out_specs=pl.BlockSpec((rows, block), lambda n, order: (0, n)),
        ),
        out_shape=jax.ShapeDtypeStruct((rows, width), jnp.bfloat16),
        cost_estimate=pl.CostEstimate(
            flops=8 * rows * depth * width, bytes_accessed=8 * depth * width, transcendentals=0
        ),
        name="project",
    )(order, *parts, weight, weight, weight, weight)


def per_device(resid, streams, filt, q_gain, k_gain, out_weight, contig_lengths):
    resid_own = resid[0]
    streams_own = jnp.transpose(streams[0], (0, 2, 1, 3))
    rows = resid_own.shape[1]
    section = lax.axis_index("pipe")
    seq = lax.axis_index("seq")
    tensor = lax.axis_index("tensor")
    n_seq = lax.axis_size("seq")
    n_tensor = lax.axis_size("tensor")
    core = seq % 2
    y_low = (seq // 2) % 2

    half = out_weight.shape[1] // 2
    gathered = [
        lax.all_gather(out_weight[:, i * half : (i + 1) * half], "seq", axis=0, tiled=True) for i in range(2)
    ]

    tail = tail_of(streams_own)
    prev = shifted(tail, "seq", [(s, s + 1) for s in range(n_seq - 1)])
    hidden_1, attend_1 = hyena(streams_own, resid_own, prev, filt, 1)
    arrived = shifted(attend_1, "pipe", [(0, 1)])
    hidden_0, attend_0 = hyena(streams_own, resid_own, prev, filt, 0)
    own = jnp.where(section == 0, attend_0, arrived)

    behind_4 = shifted(own, "seq", [(s, s + 4) for s in range(n_seq - 4)])
    across = shifted(jnp.where(y_low == 0, own, behind_4), "seq", [(s, s ^ 2) for s in range(n_seq)])
    swap = [(s, s ^ 1) for s in range(n_seq)]
    beside = shifted(jnp.where(core == 0, own, behind_4), "seq", swap)
    beside_2 = shifted(across, "seq", swap)

    contig_ends = jnp.cumsum(contig_lengths, axis=1)[section]
    start = seq * rows
    query_pos = start + jnp.arange(rows, dtype=jnp.int32)
    low = jnp.max(jnp.where(contig_ends[None, :] <= query_pos[:, None], contig_ends[None, :], 0), axis=1)
    first_low = jnp.max(jnp.where(contig_ends <= start, contig_ends, 0))
    steps_back = jnp.array([0, 4, 2, 0, 0, 0, 0, 0], jnp.int32)
    odd = jnp.array([0, 0, 0, 1, 3, 0, 0, 0], jnp.int32)
    even = jnp.array([0, 0, 0, 3, 1, 0, 0, 0], jnp.int32)
    base = start - rows * (steps_back + jnp.where(core == 0, even, odd))
    meta = jnp.concatenate([base, (base + (rows - 1) >= first_low).astype(jnp.int32)])
    low = jnp.broadcast_to(low[:, None], (rows, HD)).astype(jnp.int32)
    mixed = attention(
        meta, (own, behind_4, across, beside, beside_2), low, q_gain[None, :], k_gain[None, :]
    )

    parts = [mixed] + [
        shifted(mixed, "tensor", [(t, (t + k) % n_tensor) for t in range(n_tensor)]) for k in (1, 3, 2)
    ]
    order = (tensor - jnp.array([0, 1, 3, 2], jnp.int32)) % n_tensor
    projected, returned = [], []
    for i in range(2):
        part = project(order, parts, gathered[i])
        projected.append(part)
        returned.append(shifted(part, "pipe", [(0, 1)]))
    first = jnp.where(section == 0, hidden_0, jnp.concatenate(returned, axis=1))
    second = jnp.where(section == 0, hidden_1, jnp.concatenate(projected, axis=1))
    return jnp.stack([first, second])[None]


def solution(mesh):
    placed = (
        P("pipe", None, "seq", "tensor"),
        P("pipe", None, "seq", None, "tensor"),
        P(None, "tensor"),
        P("tensor"),
        P("tensor"),
        P("seq", "tensor"),
        P(),
    )
    return jax.shard_map(
        per_device,
        mesh=mesh,
        in_specs=placed,
        out_specs=P("pipe", None, "seq", "tensor"),
        check_vma=False,
    )
```

```python
import jax
import jax.numpy as jnp
from jax import lax
from jax.experimental import pallas as pl
from jax.experimental.pallas import tpu as pltpu
from jax.sharding import PartitionSpec as P

HD = 128
NEG_FILL = -1e30
HALO = 8
COLS = 512
ROWS = 32


def shifted(value, axis, pairs):
    return lax.ppermute(value, axis, pairs)


def tail_body(stream, tail):
    for b in range(stream.shape[0]):
        gate = stream[b, 0].astype(jnp.float32) * stream[b, 2].astype(jnp.float32)
        tail[b] = gate.astype(jnp.bfloat16)


def tail_of(streams):
    batches, kinds, rows, width = streams.shape
    return pl.pallas_call(
        tail_body,
        grid=(1,),
        in_specs=[pl.BlockSpec((batches, kinds, HALO, width), lambda i: (0, 0, rows // HALO - 1, 0))],
        out_specs=pl.BlockSpec((batches, HALO, width), lambda i: (0, 0, 0)),
        out_shape=jax.ShapeDtypeStruct((batches, HALO, width), jnp.bfloat16),
        name="tail",
    )(streams)


def hyena_body(stream, resid, prev, filt, hidden, attend, extended):
    taps = filt.shape[0]
    rows, cols = resid.shape
    extended[0:HALO] = prev[...].astype(jnp.float32)
    for r in range(0, rows, ROWS):
        gate = stream[0, r : r + ROWS].astype(jnp.float32) * stream[2, r : r + ROWS].astype(jnp.float32)
        extended[HALO + r : HALO + r + ROWS] = gate.astype(jnp.bfloat16).astype(jnp.float32)
    weights = [filt[j : j + 1].astype(jnp.float32) for j in range(taps)]
    for r in range(0, rows, ROWS):
        conv = weights[0] * extended[HALO + r : HALO + r + ROWS]
        for j in range(1, taps):
            conv = conv + weights[j] * extended[HALO + r - j : HALO + r - j + ROWS]
        mixed = resid[r : r + ROWS].astype(jnp.float32) + stream[1, r : r + ROWS].astype(jnp.float32) * conv
        mixed = mixed.astype(jnp.bfloat16)
        hidden[r : r + ROWS] = mixed
        for c in range(cols // (2 * HD)):
            attend[r : r + ROWS, c * HD : (c + 1) * HD] = mixed[:, 2 * c * HD : (2 * c + 1) * HD]


def hyena(streams, resid, prev, filt, batch):
    _, _, rows, width = streams.shape
    taps = filt.shape[0]
    return pl.pallas_call(
        hyena_body,
        grid=(width // COLS,),
        in_specs=[
            pl.BlockSpec((None, 3, rows, COLS), lambda c: (batch, 0, 0, c)),
            pl.BlockSpec((None, rows, COLS), lambda c: (batch, 0, c)),
            pl.BlockSpec((None, HALO, COLS), lambda c: (batch, 0, c)),
            pl.BlockSpec((taps, COLS), lambda c: (0, c)),
        ],
        out_specs=[
            pl.BlockSpec((rows, COLS), lambda c: (0, c)),
            pl.BlockSpec((rows, COLS // 2), lambda c: (0, c)),
        ],
        out_shape=[
            jax.ShapeDtypeStruct((rows, width), jnp.bfloat16),
            jax.ShapeDtypeStruct((rows, width // 2), jnp.bfloat16),
        ],
        scratch_shapes=[pltpu.VMEM((HALO + rows, COLS), jnp.float32)],
        cost_estimate=pl.CostEstimate(flops=20 * rows * width, bytes_accessed=11 * rows * width, transcendentals=0),
        name="hyena",
    )(streams, resid, prev, filt)


def attention_body(meta, own, p1, p2, p3, p4, low, q_gain, k_gain, mixed, acc, top, total):
    rows = own.shape[0]
    query = (own[...].astype(jnp.float32) * q_gain[...]).astype(jnp.bfloat16)
    lowest = low[:, 0:1]
    row = lax.broadcasted_iota(jnp.int32, (rows, rows), 0)
    col = lax.broadcasted_iota(jnp.int32, (rows, rows), 1)

    def scores_of(piece):
        key = (piece.astype(jnp.float32) * k_gain[...]).astype(jnp.bfloat16)
        return lax.dot_general(
            query, key, (((1,), (1,)), ((), ())), preferred_element_type=jnp.float32
        ) * (1.0 / HD)

    def weighted(weights, piece):
        return jnp.dot(weights.astype(jnp.bfloat16), piece, preferred_element_type=jnp.float32)

    value = own[...]
    scores = scores_of(value)
    scores = jnp.where((col + meta[0] >= lowest) & (col <= row), scores, NEG_FILL)
    best = jnp.max(scores, axis=1, keepdims=True)
    weights = jnp.exp(scores - best)
    top[...] = best
    total[...] = jnp.sum(weights, axis=1, keepdims=True)
    acc[...] = weighted(weights, value)
    for k, ref in enumerate((p1, p2, p3, p4), 1):

        @pl.when(meta[8 + k] > 0)
        def _(k=k, ref=ref):
            piece = ref[...]
            part = jnp.where(col + meta[k] >= lowest, scores_of(piece), NEG_FILL)
            old = top[...]
            new = jnp.maximum(old, jnp.max(part, axis=1, keepdims=True))
            scale = jnp.exp(old - new)
            part = jnp.exp(part - new)
            top[...] = new
            total[...] = total[...] * scale + jnp.sum(part, axis=1, keepdims=True)
            acc[...] = acc[...] * scale + weighted(part, piece)

    mixed[...] = (acc[...] / total[...]).astype(jnp.bfloat16)


def attention(meta, pieces, low, q_gain, k_gain):
    rows, width = pieces[0].shape
    heads = width // HD
    by_head = pl.BlockSpec((rows, HD), lambda g, meta: (0, g))
    gain = pl.BlockSpec((1, HD), lambda g, meta: (0, g))
    return pl.pallas_call(
        attention_body,
        grid_spec=pltpu.PrefetchScalarGridSpec(
            num_scalar_prefetch=1,
            grid=(heads,),
            in_specs=[by_head] * 5 + [pl.BlockSpec((rows, HD), lambda g, meta: (0, 0)), gain, gain],
            out_specs=by_head,
            scratch_shapes=[
                pltpu.VMEM((rows, HD), jnp.float32),
                pltpu.VMEM((rows, 1), jnp.float32),
                pltpu.VMEM((rows, 1), jnp.float32),
            ],
        ),
        out_shape=jax.ShapeDtypeStruct((rows, width), jnp.bfloat16),
        cost_estimate=pl.CostEstimate(
            flops=4 * 5 * rows * rows * width, bytes_accessed=12 * rows * width, transcendentals=5 * rows * rows * heads
        ),
        name="attention",
    )(meta, *pieces, low, q_gain, k_gain)


def project_body(order, *refs):
    parts, weights, out = refs[:4], refs[4:12], refs[12]
    depth = weights[0].shape[0]
    total = None
    for k in range(8):
        piece = parts[k // 2][:, (k % 2) * depth : (k % 2 + 1) * depth]
        product = jnp.dot(piece, weights[k][...], preferred_element_type=jnp.float32)
        total = product if total is None else total + product
    out[...] = total.astype(jnp.bfloat16)


def project(order, parts, weight, block=256):
    rows, depth = parts[0].shape
    width = weight.shape[1]

    def w_spec(k):
        return pl.BlockSpec((depth // 2, block), lambda n, order: (order[k], n))

    return pl.pallas_call(
        project_body,
        grid_spec=pltpu.PrefetchScalarGridSpec(
            num_scalar_prefetch=1,
            grid=(width // block,),
            in_specs=[pl.BlockSpec((rows, depth), lambda n, order: (0, 0))] * 4 + [w_spec(k) for k in range(8)],
            out_specs=pl.BlockSpec((rows, block), lambda n, order: (0, n)),
        ),
        out_shape=jax.ShapeDtypeStruct((rows, width), jnp.bfloat16),
        cost_estimate=pl.CostEstimate(
            flops=8 * rows * depth * width, bytes_accessed=8 * depth * width, transcendentals=0
        ),
        name="project",
    )(order, *parts, *([weight] * 8))


def per_device(resid, streams, filt, q_gain, k_gain, out_weight, contig_lengths):
    resid_own = resid[0]
    streams_own = jnp.transpose(streams[0], (0, 2, 1, 3))
    rows = resid_own.shape[1]
    section = lax.axis_index("pipe")
    seq = lax.axis_index("seq")
    tensor = lax.axis_index("tensor")
    n_seq = lax.axis_size("seq")
    n_tensor = lax.axis_size("tensor")
    core = seq % 2
    y_low = (seq // 2) % 2

    half = out_weight.shape[1] // 2
    share = lax.dynamic_slice_in_dim(out_weight, section * half, half, 1)
    n_sections = lax.axis_size("pipe")
    torus = [p * n_seq + z * 4 + j for z in range(n_seq // 4) for p in range(n_sections) for j in range(4)]
    gathered = lax.all_gather(share, ("pipe", "seq"), axis=0, tiled=True, axis_index_groups=[torus])

    tail = tail_of(streams_own)
    prev = shifted(tail, "seq", [(s, s + 1) for s in range(n_seq - 1)])
    hidden_1, attend_1 = hyena(streams_own, resid_own, prev, filt, 1)
    arrived = shifted(attend_1, "pipe", [(0, 1)])
    hidden_0, attend_0 = hyena(streams_own, resid_own, prev, filt, 0)
    own = jnp.where(section == 0, attend_0, arrived)

    behind_4 = shifted(own, "seq", [(s, s + 4) for s in range(n_seq - 4)])
    across = shifted(jnp.where(y_low == 0, own, behind_4), "seq", [(s, s ^ 2) for s in range(n_seq)])
    swap = [(s, s ^ 1) for s in range(n_seq)]
    beside = shifted(jnp.where(core == 0, own, behind_4), "seq", swap)
    beside_2 = shifted(across, "seq", swap)

    contig_ends = jnp.cumsum(contig_lengths, axis=1)[section]
    start = seq * rows
    query_pos = start + jnp.arange(rows, dtype=jnp.int32)
    low = jnp.max(jnp.where(contig_ends[None, :] <= query_pos[:, None], contig_ends[None, :], 0), axis=1)
    first_low = jnp.max(jnp.where(contig_ends <= start, contig_ends, 0))
    steps_back = jnp.array([0, 4, 2, 0, 0, 0, 0, 0], jnp.int32)
    odd = jnp.array([0, 0, 0, 1, 3, 0, 0, 0], jnp.int32)
    even = jnp.array([0, 0, 0, 3, 1, 0, 0, 0], jnp.int32)
    base = start - rows * (steps_back + jnp.where(core == 0, even, odd))
    meta = jnp.concatenate([base, (base + (rows - 1) >= first_low).astype(jnp.int32)])
    low = jnp.broadcast_to(low[:, None], (rows, HD)).astype(jnp.int32)
    mixed = attention(
        meta, (own, behind_4, across, beside, beside_2), low, q_gain[None, :], k_gain[None, :]
    )

    parts = [mixed] + [
        shifted(mixed, "tensor", [(t, (t + k) % n_tensor) for t in range(n_tensor)]) for k in (1, 3, 2)
    ]
    sources = (tensor - jnp.array([0, 0, 1, 1, 3, 3, 2, 2], jnp.int32)) % n_tensor
    order = (2 * sources + jnp.array([0, 1] * 4, jnp.int32)) * n_sections
    projected, returned = [], []
    for i in range(2):
        part = project(order + i, parts, gathered)
        projected.append(part)
        returned.append(shifted(part, "pipe", [(0, 1)]))
    first = jnp.where(section == 0, hidden_0, jnp.concatenate(returned, axis=1))
    second = jnp.where(section == 0, hidden_1, jnp.concatenate(projected, axis=1))
    return jnp.stack([first, second])[None]


def solution(mesh):
    placed = (
        P("pipe", None, "seq", "tensor"),
        P("pipe", None, "seq", None, "tensor"),
        P(None, "tensor"),
        P("tensor"),
        P("tensor"),
        P("seq", "tensor"),
        P(),
    )
    return jax.shard_map(
        per_device,
        mesh=mesh,
        in_specs=placed,
        out_specs=P("pipe", None, "seq", "tensor"),
        check_vma=False,
    )
```

```python
import functools

import jax
import jax.numpy as jnp
from jax import lax
from jax.experimental import pallas as pl
from jax.experimental.pallas import tpu as pltpu
from jax.sharding import PartitionSpec as P

HD = 128
NEG_FILL = -1e30
HALO = 8
COLS = 512
ROWS = 32
TILE = 128
GROUP = 4


def shifted(value, axis, pairs):
    return lax.ppermute(value, axis, pairs)


def tail_body(stream, tail):
    for b in range(stream.shape[0]):
        gate = stream[b, 0].astype(jnp.float32) * stream[b, 2].astype(jnp.float32)
        tail[b] = gate.astype(jnp.bfloat16)


def tail_of(streams):
    batches, kinds, rows, width = streams.shape
    return pl.pallas_call(
        tail_body,
        grid=(1,),
        in_specs=[pl.BlockSpec((batches, kinds, HALO, width), lambda i: (0, 0, rows // HALO - 1, 0))],
        out_specs=pl.BlockSpec((batches, HALO, width), lambda i: (0, 0, 0)),
        out_shape=jax.ShapeDtypeStruct((batches, HALO, width), jnp.bfloat16),
        name="tail",
    )(streams)


def hyena_body(stream, resid, prev, filt, hidden, attend, extended):
    taps = filt.shape[0]
    rows, cols = resid.shape
    extended[0:HALO] = prev[...].astype(jnp.float32)
    for r in range(0, rows, ROWS):
        gate = stream[0, r : r + ROWS].astype(jnp.float32) * stream[2, r : r + ROWS].astype(jnp.float32)
        extended[HALO + r : HALO + r + ROWS] = gate.astype(jnp.bfloat16).astype(jnp.float32)
    weights = [filt[j : j + 1].astype(jnp.float32) for j in range(taps)]
    for r in range(0, rows, ROWS):
        conv = weights[0] * extended[HALO + r : HALO + r + ROWS]
        for j in range(1, taps):
            conv = conv + weights[j] * extended[HALO + r - j : HALO + r - j + ROWS]
        mixed = resid[r : r + ROWS].astype(jnp.float32) + stream[1, r : r + ROWS].astype(jnp.float32) * conv
        mixed = mixed.astype(jnp.bfloat16)
        hidden[r : r + ROWS] = mixed
        for c in range(cols // (2 * HD)):
            attend[r : r + ROWS, c * HD : (c + 1) * HD] = mixed[:, 2 * c * HD : (2 * c + 1) * HD]


def hyena(streams, resid, prev, filt, batch):
    _, _, rows, width = streams.shape
    taps = filt.shape[0]
    return pl.pallas_call(
        hyena_body,
        grid=(width // COLS,),
        in_specs=[
            pl.BlockSpec((None, 3, rows, COLS), lambda c: (batch, 0, 0, c)),
            pl.BlockSpec((None, rows, COLS), lambda c: (batch, 0, c)),
            pl.BlockSpec((None, HALO, COLS), lambda c: (batch, 0, c)),
            pl.BlockSpec((taps, COLS), lambda c: (0, c)),
        ],
        out_specs=[
            pl.BlockSpec((rows, COLS), lambda c: (0, c)),
            pl.BlockSpec((rows, COLS // 2), lambda c: (0, c)),
        ],
        out_shape=[
            jax.ShapeDtypeStruct((rows, width), jnp.bfloat16),
            jax.ShapeDtypeStruct((rows, width // 2), jnp.bfloat16),
        ],
        scratch_shapes=[pltpu.VMEM((HALO + rows, COLS), jnp.float32)],
        cost_estimate=pl.CostEstimate(flops=20 * rows * width, bytes_accessed=11 * rows * width, transcendentals=0),
        name="hyena",
    )(streams, resid, prev, filt)


def attention_body(meta, *refs):
    low, q_gain, k_gain, mixed = refs[10:14]
    pieces = refs[14:19]
    rows, width = pieces[0].shape
    odd = meta[6]
    for section in range(2):

        @pl.when(meta[7] == section)
        def _(section=section):
            own, far, mid, side_a, side_b = refs[section:10:2]
            pieces[0][...] = own[...]
            pieces[2][...] = mid[...]
            pieces[4][...] = far[...]

            @pl.when(odd == 0)
            def _():
                pieces[1][...] = side_b[...]
                pieces[3][...] = side_a[...]

            @pl.when(odd != 0)
            def _():
                pieces[1][...] = side_a[...]
                pieces[3][...] = side_b[...]

    ones = jnp.ones((rows, HD), jnp.bfloat16)
    col = lax.broadcasted_iota(jnp.int32, (TILE, rows), 1)
    row = lax.broadcasted_iota(jnp.int32, (TILE, rows), 0)

    def attend(count):
        for h in range(GROUP):
            lanes = slice(h * HD, (h + 1) * HD)
            query = (pieces[0][:, lanes].astype(jnp.float32) * q_gain[:, lanes]).astype(jnp.bfloat16)
            keys, values = [], []
            for ref in pieces[:count]:
                piece = ref[:, lanes]
                keys.append((piece.astype(jnp.float32) * k_gain[:, lanes]).astype(jnp.bfloat16))
                values.append(jnp.concatenate([piece, ones], axis=1))
            for r in range(0, rows, TILE):
                lowest = low[r : r + TILE]
                lowest = jnp.concatenate([lowest] * (rows // HD), axis=1)
                scores = []
                for k in range(count):
                    part = lax.dot_general(
                        query[r : r + TILE],
                        keys[k],
                        (((1,), (1,)), ((), ())),
                        preferred_element_type=jnp.float32,
                    )
                    seen = col >= lowest - meta[k]
                    if k == 0:
                        seen = seen & (col <= row + r)
                    scores.append(jnp.where(seen, part, NEG_FILL))
                top = scores[0]
                for part in scores[1:]:
                    top = jnp.maximum(top, part)
                top = jnp.max(top, axis=1, keepdims=True)
                acc = None
                for k in range(count):
                    weights = jnp.exp(scores[k] - top).astype(jnp.bfloat16)
                    product = jnp.dot(weights, values[k], preferred_element_type=jnp.float32)
                    acc = product if acc is None else acc + product
                out = (acc[:, :HD] / acc[:, HD:]).astype(jnp.bfloat16)
                mixed[(h % 2 + odd) % 2, r : r + TILE, (h // 2) * HD : (h // 2 + 1) * HD] = out

    for count in range(1, 6):

        @pl.when(meta[5] == count)
        def _(count=count):
            attend(count)


def attention(meta, pieces, low, q_gain, k_gain):
    rows, width = pieces[0].shape
    lanes = GROUP * HD
    by_group = pl.BlockSpec((rows, lanes), lambda g, meta: (0, g))
    gain = pl.BlockSpec((1, lanes), lambda g, meta: (0, g))
    return pl.pallas_call(
        attention_body,
        grid_spec=pltpu.PrefetchScalarGridSpec(
            num_scalar_prefetch=1,
            grid=(width // lanes,),
            in_specs=[by_group] * 10 + [pl.BlockSpec((rows, HD), lambda g, meta: (0, 0)), gain, gain],
            out_specs=pl.BlockSpec((2, rows, lanes // 2), lambda g, meta: (0, 0, g)),
            scratch_shapes=[pltpu.VMEM((rows, lanes), jnp.bfloat16)] * 5,
        ),
        out_shape=jax.ShapeDtypeStruct((2, rows, width // 2), jnp.bfloat16),
        cost_estimate=pl.CostEstimate(
            flops=2 * 5 * rows * rows * width, bytes_accessed=22 * rows * width, transcendentals=5 * rows * rows * width // HD
        ),
        name="attention",
    )(meta, *pieces, low, q_gain, k_gain)


def project_body(meta, *refs, half, chunk):
    parts, weights, (own, other) = refs[:8], refs[8:24], refs[24:26]
    left, right, sems = refs[26:29]
    n_rows = parts[0].shape[0]
    depth = weights[0].shape[0]
    width = own.shape[1]
    steps = width // chunk

    def copy(k, n):
        return pltpu.make_async_copy(
            weights[k].at[:, pl.ds(half * width + n * chunk, chunk)],
            right.at[n, pl.ds(k * depth, depth)],
            sems.at[n, k],
        )

    for n in range(steps):
        for k in range(16):
            copy(k, n).start()
    z, tensor, y_low = meta[0], meta[1], meta[2]
    for rel, shift in enumerate((0, 1, 3, 2)):
        for zz in range(2):
            slot = (z - (2 * ((tensor + 4 - shift) % 4) + zz) + 8) % 8
            for side in range(2):
                ref = parts[2 * rel + side]
                rows = slice(side * n_rows, (side + 1) * n_rows)

                @pl.when(y_low == 0)
                def _(slot=slot, ref=ref, rows=rows, zz=zz):
                    left[slot, rows] = ref[:, 2 * zz * depth : (2 * zz + 2) * depth]

                @pl.when(y_low != 0)
                def _(slot=slot, ref=ref, rows=rows, zz=zz):
                    left[slot, rows, 0:depth] = ref[:, (2 * zz + 1) * depth : (2 * zz + 2) * depth]
                    left[slot, rows, depth : 2 * depth] = ref[:, 2 * zz * depth : (2 * zz + 1) * depth]

    whole = jnp.concatenate([left[k] for k in range(8)], axis=1)
    for n in range(steps):
        for k in range(16):
            copy(k, n).wait()
        total = jnp.dot(whole, right[n], preferred_element_type=jnp.float32)
        own[:, n * chunk : (n + 1) * chunk] = total[:n_rows]
        other[:, n * chunk : (n + 1) * chunk] = total[n_rows:]


def project(meta, parts, weights, half, chunk=512):
    rows, lanes = parts[0].shape
    depth, width = weights[0].shape
    width = width // 2
    whole = pl.BlockSpec((rows, lanes), lambda i, meta: (0, 0))
    out = pl.BlockSpec((rows, width), lambda i, meta: (0, 0))
    result = jax.ShapeDtypeStruct((rows, width), jnp.float32)
    return pl.pallas_call(
        functools.partial(project_body, half=half, chunk=chunk),
        grid_spec=pltpu.PrefetchScalarGridSpec(
            num_scalar_prefetch=1,
            grid=(1,),
            in_specs=[whole] * 8 + [pl.BlockSpec(memory_space=pl.ANY)] * 16,
            out_specs=[out, out],
            scratch_shapes=[
                pltpu.VMEM((8, 2 * rows, 2 * depth), jnp.bfloat16),
                pltpu.VMEM((width // chunk, 16 * depth, chunk), jnp.bfloat16),
                pltpu.SemaphoreType.DMA((width // chunk, 16)),
            ],
        ),
        out_shape=[result, result],
        cost_estimate=pl.CostEstimate(
            flops=2 * 2 * rows * 16 * depth * width, bytes_accessed=32 * depth * width, transcendentals=0
        ),
        name="project",
    )(meta, *parts, *weights)


def per_device(resid, streams, filt, q_gain, k_gain, out_weight, contig_lengths):
    resid_own = resid[0]
    streams_own = jnp.transpose(streams[0], (0, 2, 1, 3))
    rows = resid_own.shape[1]
    section = lax.axis_index("pipe")
    seq = lax.axis_index("seq")
    tensor = lax.axis_index("tensor")
    n_seq = lax.axis_size("seq")
    n_tensor = lax.axis_size("tensor")
    n_z = n_seq // 4
    core = seq % 2
    y_low = (seq // 2) % 2
    both = ("pipe", "seq")

    def along_y(value, step):
        pairs = []
        for y in range(4):
            to = (y + step) % 4
            for z in range(n_z):
                for c in range(2):
                    pairs.append(((y // 2) * n_seq + z * 4 + (y % 2) * 2 + c, (to // 2) * n_seq + z * 4 + (to % 2) * 2 + c))
        return shifted(value, both, pairs)

    def along_z(value, step):
        return shifted(value, "seq", [(s, (s + 4 * step) % n_seq) for s in range(n_seq)])

    def within(value, which, move):
        pairs = [(which * n_seq + s, which * n_seq + move(s)) for s in range(n_seq) if 0 <= move(s) < n_seq]
        return shifted(value, both, pairs)

    def along_tensor(value, step):
        return shifted(value, "tensor", [(t, (t + step) % n_tensor) for t in range(n_tensor)])

    tail = tail_of(streams_own)
    prev = shifted(tail, "seq", [(s, s + 1) for s in range(n_seq - 1)])
    hidden_0, attend_0 = hyena(streams_own, resid_own, prev, filt, 0)
    hidden_1, attend_1 = hyena(streams_own, resid_own, prev, filt, 1)
    arrived = shifted(attend_1, "pipe", [(0, 1)])

    right, left = [out_weight], [out_weight]
    across = {0: along_y(out_weight, 1)}
    for k in range(1, 5):
        right.append(along_z(right[-1], 1))
        across[k] = along_y(right[k], 1 if k < 4 else -1)
        if k < 4:
            left.append(along_z(left[-1], -1))
            across[8 - k] = along_y(left[k], -1)
    same = right + [left[k] for k in (3, 2, 1)]
    weights = []
    for k in range(8):
        weights += [same[k], across[k]]

    pieces = []
    for which, own in ((0, attend_0), (1, arrived)):
        behind = within(own, which, lambda s: s + 4)
        beside = within(jnp.where(core == 0, own, behind), which, lambda s: s ^ 1)
        mid = within(jnp.where(y_low == 0, own, behind), which, lambda s: s ^ 2)
        beside_2 = within(mid, which, lambda s: s ^ 1)
        pieces.append((own, behind, mid, beside, beside_2))
    pieces = [value for pair in zip(*pieces) for value in pair]

    contig_ends = jnp.cumsum(contig_lengths, axis=1)[section]
    start = seq * rows
    query_pos = start + jnp.arange(rows, dtype=jnp.int32)
    low = jnp.max(jnp.where(contig_ends[None, :] <= query_pos[:, None], contig_ends[None, :], 0), axis=1)
    first_low = jnp.max(jnp.where(contig_ends <= start, contig_ends, 0))
    count = 1 + (start - first_low + rows - 1) // rows
    slots = jnp.arange(8, dtype=jnp.int32)
    meta = jnp.where(slots < 5, start - rows * slots, 0)
    meta = jnp.where(slots == 5, count, jnp.where(slots == 6, core, jnp.where(slots == 7, section, meta)))
    low = jnp.broadcast_to(low[:, None], (rows, HD)).astype(jnp.int32)
    mixed = attention(meta, pieces, low, q_gain[None, :] * (1.0 / HD), k_gain[None, :])

    keep = mixed[0]
    got = shifted(mixed[1], "seq", [(s, s ^ 1) for s in range(n_seq)])
    keep_1, keep_3 = along_tensor(keep, 1), along_tensor(keep, -1)
    got_1, got_3 = along_tensor(got, 1), along_tensor(got, -1)
    keep_2, got_2 = along_tensor(keep_1, 1), along_tensor(got_3, -1)
    parts = [keep, got, keep_1, got_1, keep_3, got_3, keep_2, got_2]
    place = jnp.where(slots == 0, seq // 4, jnp.where(slots == 1, tensor, y_low))
    projected, returned = [], []
    for half in range(2):
        own, other = project(place, parts, weights, half)
        other = shifted(other, "seq", [(s, s ^ 1) for s in range(n_seq)])
        part = (own + other).astype(jnp.bfloat16)
        projected.append(part)
        returned.append(shifted(part, "pipe", [(0, 1)]))
    first = jnp.where(section == 0, hidden_0, jnp.concatenate(returned, axis=1))
    second = jnp.where(section == 0, hidden_1, jnp.concatenate(projected, axis=1))
    return jnp.stack([first, second])[None]


def solution(mesh):
    placed = (
        P("pipe", None, "seq", "tensor"),
        P("pipe", None, "seq", None, "tensor"),
        P(None, "tensor"),
        P("tensor"),
        P("tensor"),
        P("seq", "tensor"),
        P(),
    )
    return jax.shard_map(
        per_device,
        mesh=mesh,
        in_specs=placed,
        out_specs=P("pipe", None, "seq", "tensor"),
        check_vma=False,
    )
```

```python
import functools

import jax
import jax.numpy as jnp
from jax import lax
from jax.experimental import pallas as pl
from jax.experimental.pallas import tpu as pltpu
from jax.sharding import PartitionSpec as P


HD = 128
NEG_FILL = -1e30
HALO = 8
COLS = 512
ROWS = 32
TILE = 128
GROUP = 4


QUARTERS = 4


def tail_body(stream, tail):
    for b in range(stream.shape[0]):
        gate = stream[b, 0].astype(jnp.float32) * stream[b, 2].astype(jnp.float32)
        tail[b] = gate.astype(jnp.bfloat16)


def tail_of(streams):
    batches, kinds, rows, width = streams.shape
    return pl.pallas_call(
        tail_body,
        grid=(1,),
        in_specs=[pl.BlockSpec((batches, kinds, HALO, width), lambda i: (0, 0, rows // HALO - 1, 0))],
        out_specs=pl.BlockSpec((batches, HALO, width), lambda i: (0, 0, 0)),
        out_shape=jax.ShapeDtypeStruct((batches, HALO, width), jnp.bfloat16),
        name="tail",
    )(streams)


def hyena_body(stream, resid, prev, filt, *rest):
    hidden, attend, extended = rest[-3:]
    taps = filt.shape[0]
    rows, cols = resid.shape
    extended[0:HALO] = prev[...].astype(jnp.float32)
    for r in range(0, rows, ROWS):
        gate = stream[0, r : r + ROWS].astype(jnp.float32) * stream[2, r : r + ROWS].astype(jnp.float32)
        extended[HALO + r : HALO + r + ROWS] = gate.astype(jnp.bfloat16).astype(jnp.float32)
    weights = [filt[j : j + 1].astype(jnp.float32) for j in range(taps)]
    for r in range(0, rows, ROWS):
        conv = weights[0] * extended[HALO + r : HALO + r + ROWS]
        for j in range(1, taps):
            conv = conv + weights[j] * extended[HALO + r - j : HALO + r - j + ROWS]
        mixed = resid[r : r + ROWS].astype(jnp.float32) + stream[1, r : r + ROWS].astype(jnp.float32) * conv
        mixed = mixed.astype(jnp.bfloat16)
        hidden[r : r + ROWS] = mixed
        for c in range(cols // (2 * HD)):
            attend[r : r + ROWS, c * HD : (c + 1) * HD] = mixed[:, 2 * c * HD : (2 * c + 1) * HD]


def hyena(streams, resid, prev, filt, batch, into=None):
    batches, _, rows, width = streams.shape
    taps = filt.shape[0]
    extra = [] if into is None else [into]
    return pl.pallas_call(
        hyena_body,
        grid=(width // COLS,),
        in_specs=[
            pl.BlockSpec((None, 3, rows, COLS), lambda c: (batch, 0, 0, c)),
            pl.BlockSpec((None, rows, COLS), lambda c: (batch, 0, c)),
            pl.BlockSpec((None, HALO, COLS), lambda c: (batch, 0, c)),
            pl.BlockSpec((taps, COLS), lambda c: (0, c)),
        ]
        + [pl.BlockSpec(memory_space=pl.ANY)] * len(extra),
        out_specs=[
            pl.BlockSpec((None, rows, COLS), lambda c: (batch, 0, c)),
            pl.BlockSpec((rows, COLS // 2), lambda c: (0, c)),
        ],
        out_shape=[
            jax.ShapeDtypeStruct((batches, rows, width), jnp.bfloat16),
            jax.ShapeDtypeStruct((rows, width // 2), jnp.bfloat16),
        ],
        scratch_shapes=[pltpu.VMEM((HALO + rows, COLS), jnp.float32)],
        input_output_aliases={4: 0} if extra else {},
        cost_estimate=pl.CostEstimate(flops=20 * rows * width, bytes_accessed=11 * rows * width, transcendentals=0),
        name="hyena",
    )(streams, resid, prev, filt, *extra)


def attention_body(meta, *refs):
    own, far, mid, side_a, side_b, low, q_gain, k_gain, keep, give, mixed, near, third, query, key = refs
    rows, _ = own.shape
    odd = meta[6]

    @pl.when(odd == 0)
    def _():
        near[...] = side_b[...]
        third[...] = side_a[...]

    @pl.when(odd != 0)
    def _():
        near[...] = side_a[...]
        third[...] = side_b[...]

    pieces = (own, near, mid, third, far)
    ones = jnp.ones((rows, HD), jnp.bfloat16)
    col = lax.broadcasted_iota(jnp.int32, (TILE, rows), 1)
    row = lax.broadcasted_iota(jnp.int32, (TILE, rows), 0)

    def attend(count):
        for h in range(GROUP):
            lanes = slice(h * HD, (h + 1) * HD)
            query[:, lanes] = (own[:, lanes].astype(jnp.float32) * q_gain[:, lanes]).astype(jnp.bfloat16)
            for k, ref in enumerate(pieces[:count]):
                key[k, :, lanes] = (ref[:, lanes].astype(jnp.float32) * k_gain[:, lanes]).astype(jnp.bfloat16)

        def tile(t, carry):
            r = pl.multiple_of(t * TILE, TILE)
            lowest = low[pl.ds(r, TILE)]
            lowest = jnp.concatenate([lowest] * (rows // HD), axis=1)
            for h in range(GROUP):
                lanes = slice(h * HD, (h + 1) * HD)
                scores = []
                for k in range(count):
                    part = lax.dot_general(
                        query[pl.ds(r, TILE), lanes],
                        key[k, :, lanes],
                        (((1,), (1,)), ((), ())),
                        preferred_element_type=jnp.float32,
                    )
                    seen = col >= lowest - meta[k]
                    if k == 0:
                        seen = seen & (col <= row + r)
                    scores.append(jnp.where(seen, part, NEG_FILL))
                top = scores[0]
                for part in scores[1:]:
                    top = jnp.maximum(top, part)
                top = jnp.max(top, axis=1, keepdims=True)
                acc = None
                for k in range(count):
                    weights = jnp.exp(scores[k] - top).astype(jnp.bfloat16)
                    value = jnp.concatenate([pieces[k][:, lanes], ones], axis=1)
                    product = jnp.dot(weights, value, preferred_element_type=jnp.float32)
                    acc = product if acc is None else acc + product
                out = (acc[:, :HD] / acc[:, HD:]).astype(jnp.bfloat16)
                mixed[(h % 2 + odd) % 2, pl.ds(r, TILE), (h // 2) * HD : (h // 2 + 1) * HD] = out
            return carry

        lax.fori_loop(0, rows // TILE, tile, 0)

    for count in range(1, 6):

        @pl.when(meta[5] == count)
        def _(count=count):
            attend(count)

    keep[...] = mixed[0]
    give[...] = mixed[1]


def attention(meta, pieces, low, q_gain, k_gain):
    rows, width = pieces[0].shape
    lanes = GROUP * HD
    by_group = pl.BlockSpec((rows, lanes), lambda g, meta: (0, g))
    gain = pl.BlockSpec((1, lanes), lambda g, meta: (0, g))
    return pl.pallas_call(
        attention_body,
        grid_spec=pltpu.PrefetchScalarGridSpec(
            num_scalar_prefetch=1,
            grid=(width // lanes,),
            in_specs=[by_group] * 5 + [pl.BlockSpec((rows, HD), lambda g, meta: (0, 0)), gain, gain],
            out_specs=[pl.BlockSpec((rows, lanes // 2), lambda g, meta: (0, g))] * 2,
            scratch_shapes=[pltpu.VMEM((2, rows, lanes // 2), jnp.bfloat16)]
            + [pltpu.VMEM((rows, lanes), jnp.bfloat16)] * 3
            + [pltpu.VMEM((5, rows, lanes), jnp.bfloat16)],
        ),
        out_shape=[jax.ShapeDtypeStruct((rows, width // 2), jnp.bfloat16)] * 2,
        cost_estimate=pl.CostEstimate(
            flops=2 * 5 * rows * rows * width, bytes_accessed=12 * rows * width, transcendentals=5 * rows * rows * width // HD
        ),
        name="attention",
    )(meta, *pieces, low, q_gain, k_gain)


def stage_body(*refs):
    weights, staged, sems = refs[:16], refs[16], refs[17]
    depth = weights[0].shape[0]
    copies = [
        pltpu.make_async_copy(weights[k], staged.at[pl.ds(k * depth, depth)], sems.at[k]) for k in range(len(weights))
    ]
    for copy in copies:
        copy.start()
    for copy in copies:
        copy.wait()


def stage(weights):
    depth, width = weights[0].shape
    count = len(weights)
    return pl.pallas_call(
        stage_body,
        in_specs=[pl.BlockSpec(memory_space=pl.ANY)] * count,
        out_specs=pl.BlockSpec(memory_space=pltpu.VMEM),
        out_shape=jax.ShapeDtypeStruct((count * depth, width), jnp.bfloat16),
        scratch_shapes=[pltpu.SemaphoreType.DMA((count,))],
        compiler_params=pltpu.CompilerParams(vmem_limit_bytes=4 << 20),
        cost_estimate=pl.CostEstimate(flops=0, bytes_accessed=4 * count * depth * width, transcendentals=0),
        name="stage",
    )(*weights)


def arrange(meta, parts, left):
    n_rows = parts[0].shape[0]
    depth = parts[0].shape[1] // 4
    z, tensor, y_low = meta[0], meta[1], meta[2]
    for rel, shift in enumerate((0, 1, 3, 2)):
        for zz in range(2):
            slot = (z - (2 * ((tensor + 4 - shift) % 4) + zz) + 8) % 8
            for side in range(2):
                ref = parts[2 * rel + side]
                rows = slice(side * n_rows, (side + 1) * n_rows)

                @pl.when(y_low == 0)
                def _(slot=slot, ref=ref, rows=rows, zz=zz):
                    left[slot, rows] = ref[:, 2 * zz * depth : (2 * zz + 2) * depth]

                @pl.when(y_low != 0)
                def _(slot=slot, ref=ref, rows=rows, zz=zz):
                    left[slot, rows, 0:depth] = ref[:, (2 * zz + 1) * depth : (2 * zz + 2) * depth]
                    left[slot, rows, depth : 2 * depth] = ref[:, 2 * zz * depth : (2 * zz + 1) * depth]


def multiply(left, staged, own, other, quarter):
    n_rows, width = own.shape
    whole = jnp.concatenate([left[k] for k in range(8)], axis=1)
    total = jnp.dot(
        whole, staged[:, quarter * width : (quarter + 1) * width], preferred_element_type=jnp.float32
    )
    own[...] = total[:n_rows]
    other[...] = total[n_rows:]


def first_body(meta, *refs):
    parts, (staged, own, other, left) = refs[:8], refs[8:]
    arrange(meta, parts, left)
    multiply(left, staged, own, other, 0)


def later_body(left, staged, own, other, quarter):
    multiply(left, staged, own, other, quarter)


def project(meta, parts, staged, quarter, left=None):
    rows, lanes = parts[0].shape
    depth, width = staged.shape
    width = width // QUARTERS
    vmem = pl.BlockSpec(memory_space=pltpu.VMEM)
    result = jax.ShapeDtypeStruct((rows, width), jnp.float32)
    options = dict(
        compiler_params=pltpu.CompilerParams(vmem_limit_bytes=12 << 20),
        cost_estimate=pl.CostEstimate(
            flops=4 * rows * depth * width, bytes_accessed=2 * depth * width, transcendentals=0
        ),
        name="project",
    )
    if left is None:
        return pl.pallas_call(
            first_body,
            in_specs=[pl.BlockSpec(memory_space=pltpu.SMEM)] + [vmem] * 9,
            out_specs=[vmem] * 3,
            out_shape=[result, result, jax.ShapeDtypeStruct((8, 2 * rows, lanes // 2), jnp.bfloat16)],
            **options,
        )(meta, *parts, staged)
    return pl.pallas_call(
        functools.partial(later_body, quarter=quarter),
        in_specs=[vmem] * 2,
        out_specs=[vmem] * 2,
        out_shape=[result, result],
        **options,
    )(left, staged)


def per_device(resid, streams, filt, q_gain, k_gain, out_weight, contig_lengths):
    resid_own = resid[0]
    streams_own = jnp.transpose(streams[0], (0, 2, 1, 3))
    rows = resid_own.shape[1]
    section = lax.axis_index("pipe")
    seq = lax.axis_index("seq")
    tensor = lax.axis_index("tensor")
    n_seq = lax.axis_size("seq")
    n_tensor = lax.axis_size("tensor")
    n_z = n_seq // 4
    core = seq % 2
    y_low = (seq // 2) % 2
    both = ("pipe", "seq")

    def along_y(value, step):
        pairs = []
        for y in range(4):
            to = (y + step) % 4
            for z in range(n_z):
                for c in range(2):
                    pairs.append(((y // 2) * n_seq + z * 4 + (y % 2) * 2 + c, (to // 2) * n_seq + z * 4 + (to % 2) * 2 + c))
        return lax.ppermute(value, both, pairs)

    def along_z(value, step):
        return lax.ppermute(value, "seq", [(s, (s + 4 * step) % n_seq) for s in range(n_seq)])

    def along_tensor(value, step):
        return lax.ppermute(value, "tensor", [(t, (t + step) % n_tensor) for t in range(n_tensor)])

    partner = [(s, s ^ 1) for s in range(n_seq)]
    tail = tail_of(streams_own)
    prev = lax.ppermute(tail, "seq", [(s, s + 1) for s in range(n_seq - 1)])
    output, attend_1 = hyena(streams_own, resid_own, prev, filt, 1)
    arrived = lax.ppermute(attend_1, "pipe", [(0, 1)])
    output, attend_0 = hyena(streams_own, resid_own, prev, filt, 0, output)

    right, left = [out_weight], [out_weight]
    across = {0: along_y(out_weight, 1)}
    for k in range(1, 5):
        right.append(along_z(right[-1], 1))
        across[k] = along_y(right[k], 1 if k < 4 else -1)
        if k < 4:
            left.append(along_z(left[-1], -1))
            across[8 - k] = along_y(left[k], -1)
    same = right + [left[k] for k in (3, 2, 1)]
    weights = []
    for k in range(8):
        weights += [same[k], across[k]]

    own = jnp.where(section == 0, attend_0, arrived)
    behind = lax.ppermute(own, "seq", [(s, s + 4) for s in range(n_seq - 4)])
    mid = lax.ppermute(jnp.where(y_low == 0, own, behind), "seq", [(s, s ^ 2) for s in range(n_seq)])
    beside = lax.ppermute(jnp.where(core == 0, own, behind), "seq", partner)
    beside_2 = lax.ppermute(mid, "seq", partner)
    pieces = (own, behind, mid, beside, beside_2)

    contig_ends = jnp.cumsum(contig_lengths, axis=1)[section]
    start = seq * rows
    query_pos = start + jnp.arange(rows, dtype=jnp.int32)
    low = jnp.max(jnp.where(contig_ends[None, :] <= query_pos[:, None], contig_ends[None, :], 0), axis=1)
    first_low = jnp.max(jnp.where(contig_ends <= start, contig_ends, 0))
    count = 1 + (start - first_low + rows - 1) // rows
    slots = jnp.arange(8, dtype=jnp.int32)
    meta = jnp.where(slots < 5, start - rows * slots, jnp.where(slots == 5, count, core))
    low = jnp.broadcast_to(low[:, None], (rows, HD)).astype(jnp.int32)
    keep, give = attention(meta, pieces, low, q_gain[None, :] * (1.0 / HD), k_gain[None, :])

    got = lax.ppermute(give, "seq", partner)
    keep_1, keep_3 = along_tensor(keep, 1), along_tensor(keep, -1)
    got_1, got_3 = along_tensor(got, 1), along_tensor(got, -1)
    keep_2, got_2 = along_tensor(keep_1, 1), along_tensor(got_3, -1)
    parts = [keep, got, keep_1, got_1, keep_3, got_3, keep_2, got_2]
    place = jnp.where(slots == 0, seq // 4, jnp.where(slots == 1, tensor, y_low))

    def put(output, batch, quarter, value):
        at = (batch, 0, quarter * value.shape[1])
        old = lax.dynamic_slice(output, at, (1,) + value.shape)
        return lax.dynamic_update_slice(output, jnp.where(section == 0, old, value[None]), at)

    staged = stage(weights)
    returned, lhs = [], None
    for quarter in range(QUARTERS):
        own, other, *rest = project(place, parts, staged, quarter, lhs)
        lhs = rest[0] if rest else lhs
        other = lax.ppermute(other, "seq", partner)
        part = (own + other).astype(jnp.bfloat16)
        returned.append(lax.ppermute(part, "pipe", [(0, 1)]))
        output = put(output, 1, quarter, part)
    for quarter in range(QUARTERS):
        output = put(output, 0, quarter, returned[quarter])
    return output[None]


def solution(mesh):
    placed = (
        P("pipe", None, "seq", "tensor"),
        P("pipe", None, "seq", None, "tensor"),
        P(None, "tensor"),
        P("tensor"),
        P("tensor"),
        P("seq", "tensor"),
        P(),
    )
    return jax.shard_map(
        per_device,
        mesh=mesh,
        in_specs=placed,
        out_specs=P("pipe", None, "seq", "tensor"),
        check_vma=False,
    )
```

```python
import functools

import jax
import jax.numpy as jnp
from jax import lax
from jax.experimental import pallas as pl
from jax.experimental.pallas import tpu as pltpu
from jax.sharding import PartitionSpec as P


HD = 128
NEG_FILL = -1e30
HALO = 8
COLS = 512
ROWS = 32
TILE = 128
GROUP = 4


HALVES = 2
CHUNK = 512


def tail_body(stream, tail):
    for b in range(stream.shape[0]):
        gate = stream[b, 0].astype(jnp.float32) * stream[b, 2].astype(jnp.float32)
        tail[b] = gate.astype(jnp.bfloat16)


def tail_of(streams):
    batches, kinds, rows, width = streams.shape
    return pl.pallas_call(
        tail_body,
        grid=(1,),
        in_specs=[pl.BlockSpec((batches, kinds, HALO, width), lambda i: (0, 0, rows // HALO - 1, 0))],
        out_specs=pl.BlockSpec((batches, HALO, width), lambda i: (0, 0, 0)),
        out_shape=jax.ShapeDtypeStruct((batches, HALO, width), jnp.bfloat16),
        name="tail",
    )(streams)


def hyena_body(stream, resid, prev, filt, *rest):
    hidden, attend, extended = rest[-3:]
    taps = filt.shape[0]
    rows, cols = resid.shape
    extended[0:HALO] = prev[...].astype(jnp.float32)
    for r in range(0, rows, ROWS):
        gate = stream[0, r : r + ROWS].astype(jnp.float32) * stream[2, r : r + ROWS].astype(jnp.float32)
        extended[HALO + r : HALO + r + ROWS] = gate.astype(jnp.bfloat16).astype(jnp.float32)
    weights = [filt[j : j + 1].astype(jnp.float32) for j in range(taps)]
    for r in range(0, rows, ROWS):
        conv = weights[0] * extended[HALO + r : HALO + r + ROWS]
        for j in range(1, taps):
            conv = conv + weights[j] * extended[HALO + r - j : HALO + r - j + ROWS]
        mixed = resid[r : r + ROWS].astype(jnp.float32) + stream[1, r : r + ROWS].astype(jnp.float32) * conv
        mixed = mixed.astype(jnp.bfloat16)
        hidden[r : r + ROWS] = mixed
        for c in range(cols // (2 * HD)):
            attend[r : r + ROWS, c * HD : (c + 1) * HD] = mixed[:, 2 * c * HD : (2 * c + 1) * HD]


def hyena(streams, resid, prev, filt, batch, into=None):
    batches, _, rows, width = streams.shape
    taps = filt.shape[0]
    extra = [] if into is None else [into]
    return pl.pallas_call(
        hyena_body,
        grid=(width // COLS,),
        in_specs=[
            pl.BlockSpec((None, 3, rows, COLS), lambda c: (batch, 0, 0, c)),
            pl.BlockSpec((None, rows, COLS), lambda c: (batch, 0, c)),
            pl.BlockSpec((None, HALO, COLS), lambda c: (batch, 0, c)),
            pl.BlockSpec((taps, COLS), lambda c: (0, c)),
        ]
        + [pl.BlockSpec(memory_space=pl.ANY)] * len(extra),
        out_specs=[
            pl.BlockSpec((None, rows, COLS), lambda c: (batch, 0, c)),
            pl.BlockSpec((rows, COLS // 2), lambda c: (0, c)),
        ],
        out_shape=[
            jax.ShapeDtypeStruct((batches, rows, width), jnp.bfloat16),
            jax.ShapeDtypeStruct((rows, width // 2), jnp.bfloat16),
        ],
        scratch_shapes=[pltpu.VMEM((HALO + rows, COLS), jnp.float32)],
        input_output_aliases={4: 0} if extra else {},
        cost_estimate=pl.CostEstimate(flops=20 * rows * width, bytes_accessed=11 * rows * width, transcendentals=0),
        name="hyena",
    )(streams, resid, prev, filt, *extra)


def attention_body(meta, *refs):
    own, far, mid, side_a, side_b, low, q_gain, k_gain, keep, give, mixed, near, third, query, key = refs
    rows, _ = own.shape
    odd = meta[6]

    @pl.when(odd == 0)
    def _():
        near[...] = side_b[...]
        third[...] = side_a[...]

    @pl.when(odd != 0)
    def _():
        near[...] = side_a[...]
        third[...] = side_b[...]

    pieces = (own, near, mid, third, far)
    ones = jnp.ones((rows, HD), jnp.bfloat16)
    col = lax.broadcasted_iota(jnp.int32, (TILE, rows), 1)
    row = lax.broadcasted_iota(jnp.int32, (TILE, rows), 0)

    def attend(count):
        for h in range(GROUP):
            lanes = slice(h * HD, (h + 1) * HD)
            query[:, lanes] = (own[:, lanes].astype(jnp.float32) * q_gain[:, lanes]).astype(jnp.bfloat16)
            for k, ref in enumerate(pieces[:count]):
                key[k, :, lanes] = (ref[:, lanes].astype(jnp.float32) * k_gain[:, lanes]).astype(jnp.bfloat16)

        def tile(t, carry):
            r = pl.multiple_of(t * TILE, TILE)
            lowest = low[pl.ds(r, TILE)]
            lowest = jnp.concatenate([lowest] * (rows // HD), axis=1)
            for h in range(GROUP):
                lanes = slice(h * HD, (h + 1) * HD)
                scores = []
                for k in range(count):
                    part = lax.dot_general(
                        query[pl.ds(r, TILE), lanes],
                        key[k, :, lanes],
                        (((1,), (1,)), ((), ())),
                        preferred_element_type=jnp.float32,
                    )
                    seen = col >= lowest - meta[k]
                    if k == 0:
                        seen = seen & (col <= row + r)
                    scores.append(jnp.where(seen, part, NEG_FILL))
                top = scores[0]
                for part in scores[1:]:
                    top = jnp.maximum(top, part)
                top = jnp.max(top, axis=1, keepdims=True)
                acc = None
                for k in range(count):
                    weights = jnp.exp(scores[k] - top).astype(jnp.bfloat16)
                    value = jnp.concatenate([pieces[k][:, lanes], ones], axis=1)
                    product = jnp.dot(weights, value, preferred_element_type=jnp.float32)
                    acc = product if acc is None else acc + product
                out = (acc[:, :HD] / acc[:, HD:]).astype(jnp.bfloat16)
                mixed[(h % 2 + odd) % 2, pl.ds(r, TILE), (h // 2) * HD : (h // 2 + 1) * HD] = out
            return carry

        lax.fori_loop(0, rows // TILE, tile, 0)

    for count in range(1, 6):

        @pl.when(meta[5] == count)
        def _(count=count):
            attend(count)

    keep[...] = mixed[0]
    give[...] = mixed[1]


def attention(meta, pieces, low, q_gain, k_gain):
    rows, width = pieces[0].shape
    lanes = GROUP * HD
    by_group = pl.BlockSpec((rows, lanes), lambda g, meta: (0, g))
    gain = pl.BlockSpec((1, lanes), lambda g, meta: (0, g))
    return pl.pallas_call(
        attention_body,
        grid_spec=pltpu.PrefetchScalarGridSpec(
            num_scalar_prefetch=1,
            grid=(width // lanes,),
            in_specs=[by_group] * 5 + [pl.BlockSpec((rows, HD), lambda g, meta: (0, 0)), gain, gain],
            out_specs=[pl.BlockSpec((rows, lanes // 2), lambda g, meta: (0, g))] * 2,
            scratch_shapes=[pltpu.VMEM((2, rows, lanes // 2), jnp.bfloat16)]
            + [pltpu.VMEM((rows, lanes), jnp.bfloat16)] * 3
            + [pltpu.VMEM((5, rows, lanes), jnp.bfloat16)],
        ),
        out_shape=[jax.ShapeDtypeStruct((rows, width // 2), jnp.bfloat16)] * 2,
        cost_estimate=pl.CostEstimate(
            flops=2 * 5 * rows * rows * width, bytes_accessed=12 * rows * width, transcendentals=5 * rows * rows * width // HD
        ),
        name="attention",
    )(meta, *pieces, low, q_gain, k_gain)


def stage_body(*refs):
    weights, staged, sems = refs[:16], refs[16], refs[17]
    depth = weights[0].shape[0]
    copies = [
        pltpu.make_async_copy(weights[k], staged.at[pl.ds(k * depth, depth)], sems.at[k]) for k in range(len(weights))
    ]
    for copy in copies:
        copy.start()
    for copy in copies:
        copy.wait()


def stage(weights):
    depth, width = weights[0].shape
    count = len(weights)
    return pl.pallas_call(
        stage_body,
        in_specs=[pl.BlockSpec(memory_space=pl.ANY)] * count,
        out_specs=pl.BlockSpec(memory_space=pltpu.VMEM),
        out_shape=jax.ShapeDtypeStruct((count * depth, width), jnp.bfloat16),
        scratch_shapes=[pltpu.SemaphoreType.DMA((count,))],
        compiler_params=pltpu.CompilerParams(vmem_limit_bytes=4 << 20),
        cost_estimate=pl.CostEstimate(flops=0, bytes_accessed=4 * count * depth * width, transcendentals=0),
        name="stage",
    )(*weights)


def arrange(meta, parts, left):
    sides = len(parts) // 4
    n_rows, lanes = parts[0].shape
    depth = lanes // 4
    z, tensor, y_low = meta[0], meta[1], meta[2]
    for rel, shift in enumerate((0, 1, 3, 2)):
        for zz in range(2):
            slot = (z - (2 * ((tensor + 4 - shift) % 4) + zz) + 8) % 8
            for side in range(sides):
                ref = parts[sides * rel + side]
                rows = slice(side * n_rows, (side + 1) * n_rows)

                @pl.when(y_low == 0)
                def _(slot=slot, ref=ref, rows=rows, zz=zz):
                    left[slot, rows] = ref[:, 2 * zz * depth : (2 * zz + 2) * depth]

                @pl.when(y_low != 0)
                def _(slot=slot, ref=ref, rows=rows, zz=zz):
                    left[slot, rows, 0:depth] = ref[:, (2 * zz + 1) * depth : (2 * zz + 2) * depth]
                    left[slot, rows, depth : 2 * depth] = ref[:, 2 * zz * depth : (2 * zz + 1) * depth]


def multiply(left, staged, own, other, begin):
    n_rows, width = own.shape

    def chunk(c, carry):
        at = pl.multiple_of(c * CHUNK, CHUNK)
        whole = jnp.concatenate([left[k] for k in range(8)], axis=1)
        total = jnp.dot(whole, staged[:, pl.ds(begin + at, CHUNK)], preferred_element_type=jnp.float32)
        own[:, pl.ds(at, CHUNK)] = total[:n_rows]
        other[:, pl.ds(at, CHUNK)] = total[n_rows:]
        return carry

    lax.fori_loop(0, width // CHUNK, chunk, 0)


def first_body(meta, *refs):
    parts, (staged, own, other, left) = refs[:-4], refs[-4:]
    arrange(meta, parts, left)
    multiply(left, staged, own, other, 0)


def later_body(left, staged, own, other, begin):
    multiply(left, staged, own, other, begin)


def project(meta, parts, staged, width, begin=0, left=None):
    rows = parts[0].shape[0] * len(parts) // 8
    lanes = parts[0].shape[1]
    depth = staged.shape[0]
    vmem = pl.BlockSpec(memory_space=pltpu.VMEM)
    result = jax.ShapeDtypeStruct((rows, width), jnp.float32)
    options = dict(
        compiler_params=pltpu.CompilerParams(vmem_limit_bytes=12 << 20),
        cost_estimate=pl.CostEstimate(
            flops=4 * rows * depth * width, bytes_accessed=2 * depth * width, transcendentals=0
        ),
        name="project",
    )
    if left is None:
        return pl.pallas_call(
            first_body,
            in_specs=[pl.BlockSpec(memory_space=pltpu.SMEM)] + [vmem] * (len(parts) + 1),
            out_specs=[vmem] * 3,
            out_shape=[result, result, jax.ShapeDtypeStruct((8, 2 * rows, lanes // 2), jnp.bfloat16)],
            **options,
        )(meta, *parts, staged)
    return pl.pallas_call(
        functools.partial(later_body, begin=begin),
        in_specs=[vmem] * 2,
        out_specs=[vmem] * 2,
        out_shape=[result, result],
        **options,
    )(left, staged)


def per_device(resid, streams, filt, q_gain, k_gain, out_weight, contig_lengths):
    resid_own = resid[0]
    streams_own = jnp.transpose(streams[0], (0, 2, 1, 3))
    rows = resid_own.shape[1]
    section = lax.axis_index("pipe")
    seq = lax.axis_index("seq")
    tensor = lax.axis_index("tensor")
    n_seq = lax.axis_size("seq")
    n_tensor = lax.axis_size("tensor")
    n_z = n_seq // 4
    core = seq % 2
    y_low = (seq // 2) % 2
    both = ("pipe", "seq")

    def along_y(value, step):
        pairs = []
        for y in range(4):
            to = (y + step) % 4
            for z in range(n_z):
                for c in range(2):
                    pairs.append(((y // 2) * n_seq + z * 4 + (y % 2) * 2 + c, (to // 2) * n_seq + z * 4 + (to % 2) * 2 + c))
        return lax.ppermute(value, both, pairs)

    def along_z(value, step):
        return lax.ppermute(value, "seq", [(s, (s + 4 * step) % n_seq) for s in range(n_seq)])

    def along_tensor(value, step):
        return lax.ppermute(value, "tensor", [(t, (t + step) % n_tensor) for t in range(n_tensor)])

    partner = [(s, s ^ 1) for s in range(n_seq)]
    tail = tail_of(streams_own)
    prev = lax.ppermute(tail, "seq", [(s, s + 1) for s in range(n_seq - 1)])
    output, attend_1 = hyena(streams_own, resid_own, prev, filt, 1)
    arrived = lax.ppermute(attend_1, "pipe", [(0, 1)])
    output, attend_0 = hyena(streams_own, resid_own, prev, filt, 0, output)

    right, left = [out_weight], [out_weight]
    across = {0: along_y(out_weight, 1)}
    for k in range(1, 5):
        right.append(along_z(right[-1], 1))
        across[k] = along_y(right[k], 1 if k < 4 else -1)
        if k < 4:
            left.append(along_z(left[-1], -1))
            across[8 - k] = along_y(left[k], -1)
    same = right + [left[k] for k in (3, 2, 1)]
    weights = []
    for k in range(8):
        weights += [same[k], across[k]]

    own = jnp.where(section == 0, attend_0, arrived)
    behind = lax.ppermute(own, "seq", [(s, s + 4) for s in range(n_seq - 4)])
    mid = lax.ppermute(jnp.where(y_low == 0, own, behind), "seq", [(s, s ^ 2) for s in range(n_seq)])
    beside = lax.ppermute(jnp.where(core == 0, own, behind), "seq", partner)
    beside_2 = lax.ppermute(mid, "seq", partner)
    pieces = (own, behind, mid, beside, beside_2)

    contig_ends = jnp.cumsum(contig_lengths, axis=1)[section]
    start = seq * rows
    query_pos = start + jnp.arange(rows, dtype=jnp.int32)
    low = jnp.max(jnp.where(contig_ends[None, :] <= query_pos[:, None], contig_ends[None, :], 0), axis=1)
    first_low = jnp.max(jnp.where(contig_ends <= start, contig_ends, 0))
    count = 1 + (start - first_low + rows - 1) // rows
    slots = jnp.arange(8, dtype=jnp.int32)
    meta = jnp.where(slots < 5, start - rows * slots, jnp.where(slots == 5, count, core))
    low = jnp.broadcast_to(low[:, None], (rows, HD)).astype(jnp.int32)
    keep, give = attention(meta, pieces, low, q_gain[None, :] * (1.0 / HD), k_gain[None, :])

    got = lax.ppermute(give, "seq", partner)
    keep_1, keep_3 = along_tensor(keep, 1), along_tensor(keep, -1)
    got_1, got_3 = along_tensor(got, 1), along_tensor(got, -1)
    split = rows // 2
    below = lax.ppermute(jnp.concatenate([keep[split:], got[split:]], axis=0), "pipe", [(0, 1)])
    keep_2, got_2 = along_tensor(keep_1, 1), along_tensor(got_3, -1)
    parts = [keep, got, keep_1, got_1, keep_3, got_3, keep_2, got_2]
    below_parts = [below] + [along_tensor(below, step) for step in (1, -1, 2)]
    place = jnp.where(slots == 0, seq // 4, jnp.where(slots == 1, tensor, y_low))

    def put(output, batch, row, col, value):
        at = (batch, row, col)
        old = lax.dynamic_slice(output, at, (1,) + value.shape)
        return lax.dynamic_update_slice(output, jnp.where(section == 0, old, value[None]), at)

    staged = stage(weights)
    width = staged.shape[1] // HALVES
    returned, lhs = [], None
    for half in range(HALVES):
        own, other, *rest = project(place, parts, staged, width, half * width, lhs)
        lhs = rest[0] if rest else lhs
        other = lax.ppermute(other, "seq", partner)
        part = (own + other).astype(jnp.bfloat16)
        returned.append(lax.ppermute(part[:split], "pipe", [(0, 1)]))
        output = put(output, 1, 0, half * width, part)
    own, other, _ = project(place, below_parts, staged, staged.shape[1])
    other = lax.ppermute(other, "seq", partner)
    output = put(output, 0, split, 0, (own + other).astype(jnp.bfloat16))
    for half in range(HALVES):
        output = put(output, 0, 0, half * width, returned[half])
    return output[None]


def solution(mesh):
    placed = (
        P("pipe", None, "seq", "tensor"),
        P("pipe", None, "seq", None, "tensor"),
        P(None, "tensor"),
        P("tensor"),
        P("tensor"),
        P("seq", "tensor"),
        P(),
    )
    return jax.shard_map(
        per_device,
        mesh=mesh,
        in_specs=placed,
        out_specs=P("pipe", None, "seq", "tensor"),
        check_vma=False,
    )
```

```python
import functools

import jax
import jax.numpy as jnp
from jax import lax
from jax.experimental import pallas as pl
from jax.experimental.pallas import tpu as pltpu
from jax.sharding import PartitionSpec as P


HD = 128
NEG_FILL = -1e30
HALO = 8
COLS = 512
ROWS = 32
TILE = 128
GROUP = 4


HALVES = 2
CHUNK = 512


def tail_body(stream, tail):
    for b in range(stream.shape[0]):
        gate = stream[b, 0].astype(jnp.float32) * stream[b, 2].astype(jnp.float32)
        tail[b] = gate.astype(jnp.bfloat16)


def tail_of(streams):
    batches, kinds, rows, width = streams.shape
    return pl.pallas_call(
        tail_body,
        grid=(1,),
        in_specs=[pl.BlockSpec((batches, kinds, HALO, width), lambda i: (0, 0, rows // HALO - 1, 0))],
        out_specs=pl.BlockSpec((batches, HALO, width), lambda i: (0, 0, 0)),
        out_shape=jax.ShapeDtypeStruct((batches, HALO, width), jnp.bfloat16),
        name="tail",
    )(streams)


def hyena_body(stream, resid, prev, filt, *rest):
    hidden, attend, extended = rest[-3:]
    taps = filt.shape[0]
    rows, cols = resid.shape
    extended[0:HALO] = prev[...].astype(jnp.float32)
    for r in range(0, rows, ROWS):
        gate = stream[0, r : r + ROWS].astype(jnp.float32) * stream[2, r : r + ROWS].astype(jnp.float32)
        extended[HALO + r : HALO + r + ROWS] = gate.astype(jnp.bfloat16).astype(jnp.float32)
    weights = [filt[j : j + 1].astype(jnp.float32) for j in range(taps)]
    for r in range(0, rows, ROWS):
        conv = weights[0] * extended[HALO + r : HALO + r + ROWS]
        for j in range(1, taps):
            conv = conv + weights[j] * extended[HALO + r - j : HALO + r - j + ROWS]
        mixed = resid[r : r + ROWS].astype(jnp.float32) + stream[1, r : r + ROWS].astype(jnp.float32) * conv
        mixed = mixed.astype(jnp.bfloat16)
        hidden[r : r + ROWS] = mixed
        for c in range(cols // (2 * HD)):
            attend[r : r + ROWS, c * HD : (c + 1) * HD] = mixed[:, 2 * c * HD : (2 * c + 1) * HD]


def hyena(streams, resid, prev, filt, batch, into=None):
    batches, _, rows, width = streams.shape
    taps = filt.shape[0]
    extra = [] if into is None else [into]
    return pl.pallas_call(
        hyena_body,
        grid=(width // COLS,),
        in_specs=[
            pl.BlockSpec((None, 3, rows, COLS), lambda c: (batch, 0, 0, c)),
            pl.BlockSpec((None, rows, COLS), lambda c: (batch, 0, c)),
            pl.BlockSpec((None, HALO, COLS), lambda c: (batch, 0, c)),
            pl.BlockSpec((taps, COLS), lambda c: (0, c)),
        ]
        + [pl.BlockSpec(memory_space=pl.ANY)] * len(extra),
        out_specs=[
            pl.BlockSpec((None, rows, COLS), lambda c: (batch, 0, c)),
            pl.BlockSpec((rows, COLS // 2), lambda c: (0, c)),
        ],
        out_shape=[
            jax.ShapeDtypeStruct((batches, rows, width), jnp.bfloat16),
            jax.ShapeDtypeStruct((rows, width // 2), jnp.bfloat16),
        ],
        scratch_shapes=[pltpu.VMEM((HALO + rows, COLS), jnp.float32)],
        input_output_aliases={4: 0} if extra else {},
        cost_estimate=pl.CostEstimate(flops=20 * rows * width, bytes_accessed=11 * rows * width, transcendentals=0),
        name="hyena",
    )(streams, resid, prev, filt, *extra)


def attention_body(meta, *refs):
    own, far, mid, side_a, side_b, low, q_gain, k_gain, keep, give, mixed, near, third, query, key = refs
    rows, _ = own.shape
    odd = meta[6]

    @pl.when(odd == 0)
    def _():
        near[...] = side_b[...]
        third[...] = side_a[...]

    @pl.when(odd != 0)
    def _():
        near[...] = side_a[...]
        third[...] = side_b[...]

    pieces = (own, near, mid, third, far)
    ones = jnp.ones((rows, HD), jnp.bfloat16)
    col = lax.broadcasted_iota(jnp.int32, (TILE, rows), 1)
    row = lax.broadcasted_iota(jnp.int32, (TILE, rows), 0)

    def attend(count):
        for h in range(GROUP):
            lanes = slice(h * HD, (h + 1) * HD)
            query[:, lanes] = (own[:, lanes].astype(jnp.float32) * q_gain[:, lanes]).astype(jnp.bfloat16)
            for k, ref in enumerate(pieces[:count]):
                key[k, :, lanes] = (ref[:, lanes].astype(jnp.float32) * k_gain[:, lanes]).astype(jnp.bfloat16)

        def tile(t, carry):
            r = pl.multiple_of(t * TILE, TILE)
            lowest = low[pl.ds(r, TILE)]
            lowest = jnp.concatenate([lowest] * (rows // HD), axis=1)
            for h in range(GROUP):
                lanes = slice(h * HD, (h + 1) * HD)
                scores = []
                for k in range(count):
                    part = lax.dot_general(
                        query[pl.ds(r, TILE), lanes],
                        key[k, :, lanes],
                        (((1,), (1,)), ((), ())),
                        preferred_element_type=jnp.float32,
                    )
                    seen = col >= lowest - meta[k]
                    if k == 0:
                        seen = seen & (col <= row + r)
                    scores.append(jnp.where(seen, part, NEG_FILL))
                top = scores[0]
                for part in scores[1:]:
                    top = jnp.maximum(top, part)
                top = jnp.max(top, axis=1, keepdims=True)
                acc = None
                for k in range(count):
                    weights = jnp.exp(scores[k] - top).astype(jnp.bfloat16)
                    value = jnp.concatenate([pieces[k][:, lanes], ones], axis=1)
                    product = jnp.dot(weights, value, preferred_element_type=jnp.float32)
                    acc = product if acc is None else acc + product
                out = (acc[:, :HD] / acc[:, HD:]).astype(jnp.bfloat16)
                mixed[(h % 2 + odd) % 2, pl.ds(r, TILE), (h // 2) * HD : (h // 2 + 1) * HD] = out
            return carry

        lax.fori_loop(0, rows // TILE, tile, 0)

    for count in range(1, 6):

        @pl.when(meta[5] == count)
        def _(count=count):
            attend(count)

    keep[...] = mixed[0]
    give[...] = mixed[1]


def attention(meta, pieces, low, q_gain, k_gain):
    rows, width = pieces[0].shape
    lanes = GROUP * HD
    by_group = pl.BlockSpec((rows, lanes), lambda g, meta: (0, g))
    gain = pl.BlockSpec((1, lanes), lambda g, meta: (0, g))
    return pl.pallas_call(
        attention_body,
        grid_spec=pltpu.PrefetchScalarGridSpec(
            num_scalar_prefetch=1,
            grid=(width // lanes,),
            in_specs=[by_group] * 5 + [pl.BlockSpec((rows, HD), lambda g, meta: (0, 0)), gain, gain],
            out_specs=[pl.BlockSpec((rows, lanes // 2), lambda g, meta: (0, g))] * 2,
            scratch_shapes=[pltpu.VMEM((2, rows, lanes // 2), jnp.bfloat16)]
            + [pltpu.VMEM((rows, lanes), jnp.bfloat16)] * 3
            + [pltpu.VMEM((5, rows, lanes), jnp.bfloat16)],
        ),
        out_shape=[jax.ShapeDtypeStruct((rows, width // 2), jnp.bfloat16)] * 2,
        cost_estimate=pl.CostEstimate(
            flops=2 * 5 * rows * rows * width, bytes_accessed=12 * rows * width, transcendentals=5 * rows * rows * width // HD
        ),
        name="attention",
    )(meta, *pieces, low, q_gain, k_gain)


def stage_body(*refs):
    weights, staged, sems = refs[:-2], refs[-2], refs[-1]
    copies, row = [], 0
    for k, ref in enumerate(weights):
        copies.append(pltpu.make_async_copy(ref, staged.at[pl.ds(row, ref.shape[0])], sems.at[k]))
        row += ref.shape[0]
    for copy in copies:
        copy.start()
    for copy in copies:
        copy.wait()


def stage(weights):
    width = weights[0].shape[1]
    depth = sum(weight.shape[0] for weight in weights)
    return pl.pallas_call(
        stage_body,
        in_specs=[pl.BlockSpec(memory_space=pl.ANY)] * len(weights),
        out_specs=pl.BlockSpec(memory_space=pltpu.VMEM),
        out_shape=jax.ShapeDtypeStruct((depth, width), jnp.bfloat16),
        scratch_shapes=[pltpu.SemaphoreType.DMA((len(weights),))],
        compiler_params=pltpu.CompilerParams(vmem_limit_bytes=4 << 20),
        cost_estimate=pl.CostEstimate(flops=0, bytes_accessed=4 * depth * width, transcendentals=0),
        name="stage",
    )(*weights)


def arrange(meta, parts, left):
    sides = len(parts) // 4
    n_rows, lanes = parts[0].shape
    depth = lanes // 4
    z, tensor, y_low = meta[0], meta[1], meta[2]
    for rel, shift in enumerate((0, 1, 3, 2)):
        for zz in range(2):
            slot = (z - (2 * ((tensor + 4 - shift) % 4) + zz) + 8) % 8
            for side in range(sides):
                ref = parts[sides * rel + side]
                rows = slice(side * n_rows, (side + 1) * n_rows)

                @pl.when(y_low == 0)
                def _(slot=slot, ref=ref, rows=rows, zz=zz):
                    left[slot, rows] = ref[:, 2 * zz * depth : (2 * zz + 2) * depth]

                @pl.when(y_low != 0)
                def _(slot=slot, ref=ref, rows=rows, zz=zz):
                    left[slot, rows, 0:depth] = ref[:, (2 * zz + 1) * depth : (2 * zz + 2) * depth]
                    left[slot, rows, depth : 2 * depth] = ref[:, 2 * zz * depth : (2 * zz + 1) * depth]


def multiply(left, staged, own, other, begin):
    n_rows, width = own.shape

    def chunk(c, carry):
        at = pl.multiple_of(c * CHUNK, CHUNK)
        whole = jnp.concatenate([left[k] for k in range(8)], axis=1)
        total = jnp.dot(whole, staged[:, pl.ds(begin + at, CHUNK)], preferred_element_type=jnp.float32)
        own[:, pl.ds(at, CHUNK)] = total[:n_rows]
        other[:, pl.ds(at, CHUNK)] = total[n_rows:]
        return carry

    lax.fori_loop(0, width // CHUNK, chunk, 0)


def first_body(meta, *refs):
    parts, (staged, own, other, left) = refs[:-4], refs[-4:]
    arrange(meta, parts, left)
    multiply(left, staged, own, other, 0)


def later_body(left, staged, own, other, begin):
    multiply(left, staged, own, other, begin)


def project(meta, parts, staged, width, begin=0, left=None):
    rows = parts[0].shape[0] * len(parts) // 8
    lanes = parts[0].shape[1]
    depth = staged.shape[0]
    vmem = pl.BlockSpec(memory_space=pltpu.VMEM)
    result = jax.ShapeDtypeStruct((rows, width), jnp.float32)
    options = dict(
        compiler_params=pltpu.CompilerParams(vmem_limit_bytes=12 << 20),
        cost_estimate=pl.CostEstimate(
            flops=4 * rows * depth * width, bytes_accessed=2 * depth * width, transcendentals=0
        ),
        name="project",
    )
    if left is None:
        return pl.pallas_call(
            first_body,
            in_specs=[pl.BlockSpec(memory_space=pltpu.SMEM)] + [vmem] * (len(parts) + 1),
            out_specs=[vmem] * 3,
            out_shape=[result, result, jax.ShapeDtypeStruct((8, 2 * rows, lanes // 2), jnp.bfloat16)],
            **options,
        )(meta, *parts, staged)
    return pl.pallas_call(
        functools.partial(later_body, begin=begin),
        in_specs=[vmem] * 2,
        out_specs=[vmem] * 2,
        out_shape=[result, result],
        **options,
    )(left, staged)


def per_device(resid, streams, filt, q_gain, k_gain, out_weight, contig_lengths):
    resid_own = resid[0]
    streams_own = jnp.transpose(streams[0], (0, 2, 1, 3))
    rows = resid_own.shape[1]
    section = lax.axis_index("pipe")
    seq = lax.axis_index("seq")
    tensor = lax.axis_index("tensor")
    n_seq = lax.axis_size("seq")
    n_tensor = lax.axis_size("tensor")
    n_z = n_seq // 4
    core = seq % 2
    y_low = (seq // 2) % 2
    both = ("pipe", "seq")

    def along_y(value, step):
        pairs = []
        for y in range(4):
            to = (y + step) % 4
            for z in range(n_z):
                for c in range(2):
                    pairs.append(((y // 2) * n_seq + z * 4 + (y % 2) * 2 + c, (to // 2) * n_seq + z * 4 + (to % 2) * 2 + c))
        return lax.ppermute(value, both, pairs)

    def along_z(value, step):
        return lax.ppermute(value, "seq", [(s, (s + 4 * step) % n_seq) for s in range(n_seq)])

    def along_tensor(value, step):
        return lax.ppermute(value, "tensor", [(t, (t + step) % n_tensor) for t in range(n_tensor)])

    partner = [(s, s ^ 1) for s in range(n_seq)]
    tail = tail_of(streams_own)
    prev = lax.ppermute(tail, "seq", [(s, s + 1) for s in range(n_seq - 1)])
    output, attend_1 = hyena(streams_own, resid_own, prev, filt, 1)
    arrived = lax.ppermute(attend_1, "pipe", [(0, 1)])
    output, attend_0 = hyena(streams_own, resid_own, prev, filt, 0, output)

    def both_ways(value):
        middle = value.shape[0] // 2
        return [along_y(value[:middle], 1), along_y(value[middle:], -1)]

    right, left = [out_weight], [out_weight]
    across = {0: both_ways(out_weight)}
    for k in range(1, 5):
        right.append(along_z(right[-1], 1))
        across[k] = [along_y(right[k], 1)] if k < 4 else both_ways(right[k])
        if k < 4:
            left.append(along_z(left[-1], -1))
            across[8 - k] = [along_y(left[k], -1)]
    same = right + [left[k] for k in (3, 2, 1)]
    weights = []
    for k in range(8):
        weights += [same[k], *across[k]]

    own = jnp.where(section == 0, attend_0, arrived)
    behind = lax.ppermute(own, "seq", [(s, s + 4) for s in range(n_seq - 4)])
    mid = lax.ppermute(jnp.where(y_low == 0, own, behind), "seq", [(s, s ^ 2) for s in range(n_seq)])
    beside = lax.ppermute(jnp.where(core == 0, own, behind), "seq", partner)
    beside_2 = lax.ppermute(mid, "seq", partner)
    pieces = (own, behind, mid, beside, beside_2)

    contig_ends = jnp.cumsum(contig_lengths, axis=1)[section]
    start = seq * rows
    query_pos = start + jnp.arange(rows, dtype=jnp.int32)
    low = jnp.max(jnp.where(contig_ends[None, :] <= query_pos[:, None], contig_ends[None, :], 0), axis=1)
    first_low = jnp.max(jnp.where(contig_ends <= start, contig_ends, 0))
    count = 1 + (start - first_low + rows - 1) // rows
    slots = jnp.arange(8, dtype=jnp.int32)
    meta = jnp.where(slots < 5, start - rows * slots, jnp.where(slots == 5, count, core))
    low = jnp.broadcast_to(low[:, None], (rows, HD)).astype(jnp.int32)
    keep, give = attention(meta, pieces, low, q_gain[None, :] * (1.0 / HD), k_gain[None, :])

    got = lax.ppermute(give, "seq", partner)
    keep_1, keep_3 = along_tensor(keep, 1), along_tensor(keep, -1)
    got_1, got_3 = along_tensor(got, 1), along_tensor(got, -1)
    split = rows // 2
    below = lax.ppermute(jnp.concatenate([keep[split:], got[split:]], axis=0), "pipe", [(0, 1)])
    keep_2, got_2 = along_tensor(keep_1, 1), along_tensor(got_3, -1)
    parts = [keep, got, keep_1, got_1, keep_3, got_3, keep_2, got_2]
    below_parts = [below] + [along_tensor(below, step) for step in (1, -1, 2)]
    place = jnp.where(slots == 0, seq // 4, jnp.where(slots == 1, tensor, y_low))

    def put(output, batch, row, col, value):
        at = (batch, row, col)
        old = lax.dynamic_slice(output, at, (1,) + value.shape)
        return lax.dynamic_update_slice(output, jnp.where(section == 0, old, value[None]), at)

    staged = stage(weights)
    width = staged.shape[1] // HALVES
    returned, lhs = [], None
    for half in range(HALVES):
        own, other, *rest = project(place, parts, staged, width, half * width, lhs)
        lhs = rest[0] if rest else lhs
        other = lax.ppermute(other, "seq", partner)
        part = (own + other).astype(jnp.bfloat16)
        returned.append(lax.ppermute(part[:split], "pipe", [(0, 1)]))
        output = put(output, 1, 0, half * width, part)
    own, other, _ = project(place, below_parts, staged, staged.shape[1])
    other = lax.ppermute(other, "seq", partner)
    output = put(output, 0, split, 0, (own + other).astype(jnp.bfloat16))
    for half in range(HALVES):
        output = put(output, 0, 0, half * width, returned[half])
    return output[None]


def solution(mesh):
    placed = (
        P("pipe", None, "seq", "tensor"),
        P("pipe", None, "seq", None, "tensor"),
        P(None, "tensor"),
        P("tensor"),
        P("tensor"),
        P("seq", "tensor"),
        P(),
    )
    return jax.shard_map(
        per_device,
        mesh=mesh,
        in_specs=placed,
        out_specs=P("pipe", None, "seq", "tensor"),
        check_vma=False,
    )
```

```python
import functools

import jax
import jax.numpy as jnp
from jax import lax
from jax.experimental import pallas as pl
from jax.experimental.pallas import tpu as pltpu
from jax.sharding import PartitionSpec as P


HD = 128
NEG_FILL = -1e30
HALO = 8
COLS = 512
ROWS = 32
TILE = 128
GROUP = 4


HALVES = 2
CHUNK = 512


def tail_body(stream, tail):
    for b in range(stream.shape[0]):
        gate = stream[b, 0].astype(jnp.float32) * stream[b, 2].astype(jnp.float32)
        tail[b] = gate.astype(jnp.bfloat16)


def tail_of(streams):
    batches, kinds, rows, width = streams.shape
    return pl.pallas_call(
        tail_body,
        grid=(1,),
        in_specs=[pl.BlockSpec((batches, kinds, HALO, width), lambda i: (0, 0, rows // HALO - 1, 0))],
        out_specs=pl.BlockSpec((batches, HALO, width), lambda i: (0, 0, 0)),
        out_shape=jax.ShapeDtypeStruct((batches, HALO, width), jnp.bfloat16),
        name="tail",
    )(streams)


def hyena_body(stream, resid, prev, filt, *rest):
    hidden, attend, extended = rest[-3:]
    taps = filt.shape[0]
    rows, cols = resid.shape
    extended[0:HALO] = prev[...].astype(jnp.float32)
    for r in range(0, rows, ROWS):
        gate = stream[0, r : r + ROWS].astype(jnp.float32) * stream[2, r : r + ROWS].astype(jnp.float32)
        extended[HALO + r : HALO + r + ROWS] = gate.astype(jnp.bfloat16).astype(jnp.float32)
    weights = [filt[j : j + 1].astype(jnp.float32) for j in range(taps)]
    for r in range(0, rows, ROWS):
        conv = weights[0] * extended[HALO + r : HALO + r + ROWS]
        for j in range(1, taps):
            conv = conv + weights[j] * extended[HALO + r - j : HALO + r - j + ROWS]
        mixed = resid[r : r + ROWS].astype(jnp.float32) + stream[1, r : r + ROWS].astype(jnp.float32) * conv
        mixed = mixed.astype(jnp.bfloat16)
        hidden[r : r + ROWS] = mixed
        for c in range(cols // (2 * HD)):
            attend[r : r + ROWS, c * HD : (c + 1) * HD] = mixed[:, 2 * c * HD : (2 * c + 1) * HD]


def hyena(streams, resid, prev, filt, batch, into=None):
    batches, _, rows, width = streams.shape
    taps = filt.shape[0]
    extra = [] if into is None else [into]
    return pl.pallas_call(
        hyena_body,
        grid=(width // COLS,),
        in_specs=[
            pl.BlockSpec((None, 3, rows, COLS), lambda c: (batch, 0, 0, c)),
            pl.BlockSpec((None, rows, COLS), lambda c: (batch, 0, c)),
            pl.BlockSpec((None, HALO, COLS), lambda c: (batch, 0, c)),
            pl.BlockSpec((taps, COLS), lambda c: (0, c)),
        ]
        + [pl.BlockSpec(memory_space=pl.ANY)] * len(extra),
        out_specs=[
            pl.BlockSpec((None, rows, COLS), lambda c: (batch, 0, c)),
            pl.BlockSpec((rows, COLS // 2), lambda c: (0, c)),
        ],
        out_shape=[
            jax.ShapeDtypeStruct((batches, rows, width), jnp.bfloat16),
            jax.ShapeDtypeStruct((rows, width // 2), jnp.bfloat16),
        ],
        scratch_shapes=[pltpu.VMEM((HALO + rows, COLS), jnp.float32)],
        input_output_aliases={4: 0} if extra else {},
        cost_estimate=pl.CostEstimate(flops=20 * rows * width, bytes_accessed=11 * rows * width, transcendentals=0),
        name="hyena",
    )(streams, resid, prev, filt, *extra)


def attention_body(meta, *refs):
    own, far, mid, side_a, side_b, low, q_gain, k_gain, keep, give, pack, mixed, near, third, query, key = refs
    rows, _ = own.shape
    odd = meta[6]

    @pl.when(odd == 0)
    def _():
        near[...] = side_b[...]
        third[...] = side_a[...]

    @pl.when(odd != 0)
    def _():
        near[...] = side_a[...]
        third[...] = side_b[...]

    pieces = (own, near, mid, third, far)
    ones = jnp.ones((rows, HD), jnp.bfloat16)
    col = lax.broadcasted_iota(jnp.int32, (TILE, rows), 1)
    row = lax.broadcasted_iota(jnp.int32, (TILE, rows), 0)

    def attend(count):
        for h in range(GROUP):
            lanes = slice(h * HD, (h + 1) * HD)
            query[:, lanes] = (own[:, lanes].astype(jnp.float32) * q_gain[:, lanes]).astype(jnp.bfloat16)
            for k, ref in enumerate(pieces[:count]):
                key[k, :, lanes] = (ref[:, lanes].astype(jnp.float32) * k_gain[:, lanes]).astype(jnp.bfloat16)

        def tile(t, carry):
            r = pl.multiple_of(t * TILE, TILE)
            lowest = low[pl.ds(r, TILE)]
            lowest = jnp.concatenate([lowest] * (rows // HD), axis=1)
            for h in range(GROUP):
                lanes = slice(h * HD, (h + 1) * HD)
                scores = []
                for k in range(count):
                    part = lax.dot_general(
                        query[pl.ds(r, TILE), lanes],
                        key[k, :, lanes],
                        (((1,), (1,)), ((), ())),
                        preferred_element_type=jnp.float32,
                    )
                    seen = col >= lowest - meta[k]
                    if k == 0:
                        seen = seen & (col <= row + r)
                    scores.append(jnp.where(seen, part, NEG_FILL))
                top = scores[0]
                for part in scores[1:]:
                    top = jnp.maximum(top, part)
                top = jnp.max(top, axis=1, keepdims=True)
                acc = None
                for k in range(count):
                    weights = jnp.exp(scores[k] - top).astype(jnp.bfloat16)
                    value = jnp.concatenate([pieces[k][:, lanes], ones], axis=1)
                    product = jnp.dot(weights, value, preferred_element_type=jnp.float32)
                    acc = product if acc is None else acc + product
                out = (acc[:, :HD] / acc[:, HD:]).astype(jnp.bfloat16)
                mixed[(h % 2 + odd) % 2, pl.ds(r, TILE), (h // 2) * HD : (h // 2 + 1) * HD] = out
            return carry

        lax.fori_loop(0, rows // TILE, tile, 0)

    for count in range(1, 6):

        @pl.when(meta[5] == count)
        def _(count=count):
            attend(count)

    keep[...] = mixed[0]
    give[...] = mixed[1]
    pack[...] = mixed[0, rows - pack.shape[0] :]


def attention(meta, pieces, low, q_gain, k_gain):
    rows, width = pieces[0].shape
    lanes = GROUP * HD
    by_group = pl.BlockSpec((rows, lanes), lambda g, meta: (0, g))
    gain = pl.BlockSpec((1, lanes), lambda g, meta: (0, g))
    return pl.pallas_call(
        attention_body,
        grid_spec=pltpu.PrefetchScalarGridSpec(
            num_scalar_prefetch=1,
            grid=(width // lanes,),
            in_specs=[by_group] * 5 + [pl.BlockSpec((rows, HD), lambda g, meta: (0, 0)), gain, gain],
            out_specs=[pl.BlockSpec((rows, lanes // 2), lambda g, meta: (0, g))] * 2
            + [pl.BlockSpec((rows // 2, lanes // 2), lambda g, meta: (0, g))],
            scratch_shapes=[pltpu.VMEM((2, rows, lanes // 2), jnp.bfloat16)]
            + [pltpu.VMEM((rows, lanes), jnp.bfloat16)] * 3
            + [pltpu.VMEM((5, rows, lanes), jnp.bfloat16)],
        ),
        out_shape=[jax.ShapeDtypeStruct((rows, width // 2), jnp.bfloat16)] * 3,
        cost_estimate=pl.CostEstimate(
            flops=2 * 5 * rows * rows * width, bytes_accessed=12 * rows * width, transcendentals=5 * rows * rows * width // HD
        ),
        name="attention",
    )(meta, *pieces, low, q_gain, k_gain)


def stage_body(*refs):
    weights, staged, sems = refs[:16], refs[16], refs[17]
    depth = weights[0].shape[0]
    copies = [
        pltpu.make_async_copy(weights[k], staged.at[pl.ds(k * depth, depth)], sems.at[k]) for k in range(len(weights))
    ]
    for copy in copies:
        copy.start()
    for copy in copies:
        copy.wait()


def stage(weights):
    depth, width = weights[0].shape
    count = len(weights)
    return pl.pallas_call(
        stage_body,
        in_specs=[pl.BlockSpec(memory_space=pl.ANY)] * count,
        out_specs=pl.BlockSpec(memory_space=pltpu.VMEM),
        out_shape=jax.ShapeDtypeStruct((count * depth, width), jnp.bfloat16),
        scratch_shapes=[pltpu.SemaphoreType.DMA((count,))],
        compiler_params=pltpu.CompilerParams(vmem_limit_bytes=4 << 20),
        cost_estimate=pl.CostEstimate(flops=0, bytes_accessed=4 * count * depth * width, transcendentals=0),
        name="stage",
    )(*weights)


def arrange(meta, parts, left):
    sides = len(parts) // 4
    n_rows, lanes = parts[0].shape
    depth = lanes // 4
    z, tensor, y_low = meta[0], meta[1], meta[2]
    for rel, shift in enumerate((0, 1, 3, 2)):
        for zz in range(2):
            slot = (z - (2 * ((tensor + 4 - shift) % 4) + zz) + 8) % 8
            for side in range(sides):
                ref = parts[sides * rel + side]
                rows = slice(side * n_rows, (side + 1) * n_rows)

                @pl.when(y_low == 0)
                def _(slot=slot, ref=ref, rows=rows, zz=zz):
                    left[slot, rows] = ref[:, 2 * zz * depth : (2 * zz + 2) * depth]

                @pl.when(y_low != 0)
                def _(slot=slot, ref=ref, rows=rows, zz=zz):
                    left[slot, rows, 0:depth] = ref[:, (2 * zz + 1) * depth : (2 * zz + 2) * depth]
                    left[slot, rows, depth : 2 * depth] = ref[:, 2 * zz * depth : (2 * zz + 1) * depth]


def multiply(left, staged, own, other, begin):
    n_rows, width = own.shape

    def chunk(c, carry):
        at = pl.multiple_of(c * CHUNK, CHUNK)
        whole = jnp.concatenate([left[k] for k in range(8)], axis=1)
        total = jnp.dot(whole, staged[:, pl.ds(begin + at, CHUNK)], preferred_element_type=jnp.float32)
        own[:, pl.ds(at, CHUNK)] = total[:n_rows]
        other[:, pl.ds(at, CHUNK)] = total[n_rows:]
        return carry

    lax.fori_loop(0, width // CHUNK, chunk, 0)


def first_body(meta, *refs):
    parts, (staged, own, other, left) = refs[:-4], refs[-4:]
    arrange(meta, parts, left)
    multiply(left, staged, own, other, 0)


def later_body(left, staged, own, other, begin):
    multiply(left, staged, own, other, begin)


def project(meta, parts, staged, width, begin=0, left=None):
    rows = parts[0].shape[0] * len(parts) // 8
    lanes = parts[0].shape[1]
    depth = staged.shape[0]
    vmem = pl.BlockSpec(memory_space=pltpu.VMEM)
    result = jax.ShapeDtypeStruct((rows, width), jnp.float32)
    options = dict(
        compiler_params=pltpu.CompilerParams(vmem_limit_bytes=12 << 20),
        cost_estimate=pl.CostEstimate(
            flops=4 * rows * depth * width, bytes_accessed=2 * depth * width, transcendentals=0
        ),
        name="project",
    )
    if left is None:
        return pl.pallas_call(
            first_body,
            in_specs=[pl.BlockSpec(memory_space=pltpu.SMEM)] + [vmem] * (len(parts) + 1),
            out_specs=[vmem] * 3,
            out_shape=[result, result, jax.ShapeDtypeStruct((8, 2 * rows, lanes // 2), jnp.bfloat16)],
            **options,
        )(meta, *parts, staged)
    return pl.pallas_call(
        functools.partial(later_body, begin=begin),
        in_specs=[vmem] * 2,
        out_specs=[vmem] * 2,
        out_shape=[result, result],
        **options,
    )(left, staged)


def per_device(resid, streams, filt, q_gain, k_gain, out_weight, contig_lengths):
    resid_own = resid[0]
    streams_own = jnp.transpose(streams[0], (0, 2, 1, 3))
    rows = resid_own.shape[1]
    section = lax.axis_index("pipe")
    seq = lax.axis_index("seq")
    tensor = lax.axis_index("tensor")
    n_seq = lax.axis_size("seq")
    n_tensor = lax.axis_size("tensor")
    n_z = n_seq // 4
    core = seq % 2
    y_low = (seq // 2) % 2
    both = ("pipe", "seq")

    def along_y(value, step):
        pairs = []
        for y in range(4):
            to = (y + step) % 4
            for z in range(n_z):
                for c in range(2):
                    pairs.append(((y // 2) * n_seq + z * 4 + (y % 2) * 2 + c, (to // 2) * n_seq + z * 4 + (to % 2) * 2 + c))
        return lax.ppermute(value, both, pairs)

    def along_z(value, step):
        return lax.ppermute(value, "seq", [(s, (s + 4 * step) % n_seq) for s in range(n_seq)])

    def along_tensor(value, step):
        return lax.ppermute(value, "tensor", [(t, (t + step) % n_tensor) for t in range(n_tensor)])

    partner = [(s, s ^ 1) for s in range(n_seq)]
    tail = tail_of(streams_own)
    prev = lax.ppermute(tail, "seq", [(s, s + 1) for s in range(n_seq - 1)])
    output, attend_1 = hyena(streams_own, resid_own, prev, filt, 1)
    arrived = lax.ppermute(attend_1, "pipe", [(0, 1)])
    output, attend_0 = hyena(streams_own, resid_own, prev, filt, 0, output)

    right, left = [out_weight], [out_weight]
    across = {0: along_y(out_weight, 1)}
    for k in range(1, 5):
        right.append(along_z(right[-1], 1))
        across[k] = along_y(right[k], 1 if k < 4 else -1)
        if k < 4:
            left.append(along_z(left[-1], -1))
            across[8 - k] = along_y(left[k], -1)
    same = right + [left[k] for k in (3, 2, 1)]
    weights = []
    for k in range(8):
        weights += [same[k], across[k]]

    own = jnp.where(section == 0, attend_0, arrived)
    behind = lax.ppermute(own, "seq", [(s, s + 4) for s in range(n_seq - 4)])
    mid = lax.ppermute(jnp.where(y_low == 0, own, behind), "seq", [(s, s ^ 2) for s in range(n_seq)])
    beside = lax.ppermute(jnp.where(core == 0, own, behind), "seq", partner)
    beside_2 = lax.ppermute(mid, "seq", partner)
    pieces = (own, behind, mid, beside, beside_2)

    contig_ends = jnp.cumsum(contig_lengths, axis=1)[section]
    start = seq * rows
    query_pos = start + jnp.arange(rows, dtype=jnp.int32)
    low = jnp.max(jnp.where(contig_ends[None, :] <= query_pos[:, None], contig_ends[None, :], 0), axis=1)
    first_low = jnp.max(jnp.where(contig_ends <= start, contig_ends, 0))
    count = 1 + (start - first_low + rows - 1) // rows
    slots = jnp.arange(8, dtype=jnp.int32)
    meta = jnp.where(slots < 5, start - rows * slots, jnp.where(slots == 5, count, core))
    low = jnp.broadcast_to(low[:, None], (rows, HD)).astype(jnp.int32)
    keep, give, pack = attention(meta, pieces, low, q_gain[None, :] * (1.0 / HD), k_gain[None, :])

    got = lax.ppermute(give, "seq", partner)
    keep_1, keep_3 = along_tensor(keep, 1), along_tensor(keep, -1)
    got_1, got_3 = along_tensor(got, 1), along_tensor(got, -1)
    split = rows // 2
    pack = lax.dynamic_update_slice(pack, got[split:], (split, 0))
    below = lax.ppermute(pack, "pipe", [(0, 1)])
    keep_2, got_2 = along_tensor(keep_1, 1), along_tensor(got_3, -1)
    parts = [keep, got, keep_1, got_1, keep_3, got_3, keep_2, got_2]
    below_parts = [below] + [along_tensor(below, step) for step in (1, -1, 2)]
    place = jnp.where(slots == 0, seq // 4, jnp.where(slots == 1, tensor, y_low))

    def put(output, batch, row, col, value):
        at = (batch, row, col)
        old = lax.dynamic_slice(output, at, (1,) + value.shape)
        return lax.dynamic_update_slice(output, jnp.where(section == 0, old, value[None]), at)

    staged = stage(weights)
    width = staged.shape[1] // HALVES
    returned, lhs = [], None
    for half in range(HALVES):
        own, other, *rest = project(place, parts, staged, width, half * width, lhs)
        lhs = rest[0] if rest else lhs
        other = lax.ppermute(other, "seq", partner)
        part = (own + other).astype(jnp.bfloat16)
        returned.append(lax.ppermute(part[:split], "pipe", [(0, 1)]))
        output = put(output, 1, 0, half * width, part)
    own, other, _ = project(place, below_parts, staged, staged.shape[1])
    other = lax.ppermute(other, "seq", partner)
    output = put(output, 0, split, 0, (own + other).astype(jnp.bfloat16))
    for half in range(HALVES):
        output = put(output, 0, 0, half * width, returned[half])
    return output[None]


def solution(mesh):
    placed = (
        P("pipe", None, "seq", "tensor"),
        P("pipe", None, "seq", None, "tensor"),
        P(None, "tensor"),
        P("tensor"),
        P("tensor"),
        P("seq", "tensor"),
        P(),
    )
    return jax.shard_map(
        per_device,
        mesh=mesh,
        in_specs=placed,
        out_specs=P("pipe", None, "seq", "tensor"),
        check_vma=False,
    )
```

```python
import functools

import jax
import jax.numpy as jnp
from jax import lax
from jax.experimental import pallas as pl
from jax.experimental.pallas import tpu as pltpu
from jax.sharding import PartitionSpec as P


HD = 128
NEG_FILL = -1e30
HALO = 8
COLS = 512
ROWS = 32
TILE = 128
GROUP = 4


HALVES = 2
CHUNK = 512


def tail_body(stream, tail):
    for b in range(stream.shape[0]):
        gate = stream[b, 0].astype(jnp.float32) * stream[b, 2].astype(jnp.float32)
        tail[b] = gate.astype(jnp.bfloat16)


def tail_of(streams):
    batches, kinds, rows, width = streams.shape
    return pl.pallas_call(
        tail_body,
        grid=(1,),
        in_specs=[pl.BlockSpec((batches, kinds, HALO, width), lambda i: (0, 0, rows // HALO - 1, 0))],
        out_specs=pl.BlockSpec((batches, HALO, width), lambda i: (0, 0, 0)),
        out_shape=jax.ShapeDtypeStruct((batches, HALO, width), jnp.bfloat16),
        name="tail",
    )(streams)


def hyena_body(stream, resid, prev, filt, *rest):
    hidden, attend, extended = rest[-3:]
    taps = filt.shape[0]
    rows, cols = resid.shape
    extended[0:HALO] = prev[...].astype(jnp.float32)
    for r in range(0, rows, ROWS):
        gate = stream[0, r : r + ROWS].astype(jnp.float32) * stream[2, r : r + ROWS].astype(jnp.float32)
        extended[HALO + r : HALO + r + ROWS] = gate.astype(jnp.bfloat16).astype(jnp.float32)
    weights = [filt[j : j + 1].astype(jnp.float32) for j in range(taps)]
    for r in range(0, rows, ROWS):
        conv = weights[0] * extended[HALO + r : HALO + r + ROWS]
        for j in range(1, taps):
            conv = conv + weights[j] * extended[HALO + r - j : HALO + r - j + ROWS]
        mixed = resid[r : r + ROWS].astype(jnp.float32) + stream[1, r : r + ROWS].astype(jnp.float32) * conv
        mixed = mixed.astype(jnp.bfloat16)
        hidden[r : r + ROWS] = mixed
        for c in range(cols // (2 * HD)):
            attend[r : r + ROWS, c * HD : (c + 1) * HD] = mixed[:, 2 * c * HD : (2 * c + 1) * HD]


def hyena(streams, resid, prev, filt, batch, into=None):
    batches, _, rows, width = streams.shape
    taps = filt.shape[0]
    extra = [] if into is None else [into]
    return pl.pallas_call(
        hyena_body,
        grid=(width // COLS,),
        in_specs=[
            pl.BlockSpec((None, 3, rows, COLS), lambda c: (batch, 0, 0, c)),
            pl.BlockSpec((None, rows, COLS), lambda c: (batch, 0, c)),
            pl.BlockSpec((None, HALO, COLS), lambda c: (batch, 0, c)),
            pl.BlockSpec((taps, COLS), lambda c: (0, c)),
        ]
        + [pl.BlockSpec(memory_space=pl.ANY)] * len(extra),
        out_specs=[
            pl.BlockSpec((None, rows, COLS), lambda c: (batch, 0, c)),
            pl.BlockSpec((rows, COLS // 2), lambda c: (0, c)),
        ],
        out_shape=[
            jax.ShapeDtypeStruct((batches, rows, width), jnp.bfloat16),
            jax.ShapeDtypeStruct((rows, width // 2), jnp.bfloat16),
        ],
        scratch_shapes=[pltpu.VMEM((HALO + rows, COLS), jnp.float32)],
        input_output_aliases={4: 0} if extra else {},
        cost_estimate=pl.CostEstimate(flops=20 * rows * width, bytes_accessed=11 * rows * width, transcendentals=0),
        name="hyena",
    )(streams, resid, prev, filt, *extra)


def attention_body(meta, *refs):
    own, far, mid, side_a, side_b, low, q_gain, k_gain, keep, give, pack, mixed, near, third, query, key = refs
    rows, _ = own.shape
    odd = meta[6]

    @pl.when(odd == 0)
    def _():
        near[...] = side_b[...]
        third[...] = side_a[...]

    @pl.when(odd != 0)
    def _():
        near[...] = side_a[...]
        third[...] = side_b[...]

    pieces = (own, near, mid, third, far)
    ones = jnp.ones((rows, HD), jnp.bfloat16)
    col = lax.broadcasted_iota(jnp.int32, (TILE, rows), 1)
    row = lax.broadcasted_iota(jnp.int32, (TILE, rows), 0)

    def attend(count):
        for h in range(GROUP):
            lanes = slice(h * HD, (h + 1) * HD)
            query[:, lanes] = (own[:, lanes].astype(jnp.float32) * q_gain[:, lanes]).astype(jnp.bfloat16)
            for k, ref in enumerate(pieces[:count]):
                key[k, :, lanes] = (ref[:, lanes].astype(jnp.float32) * k_gain[:, lanes]).astype(jnp.bfloat16)

        def tile(t, carry):
            r = pl.multiple_of(t * TILE, TILE)
            lowest = low[pl.ds(r, TILE)]
            lowest = jnp.concatenate([lowest] * (rows // HD), axis=1)
            for h in range(GROUP):
                lanes = slice(h * HD, (h + 1) * HD)
                scores = []
                for k in range(count):
                    part = lax.dot_general(
                        query[pl.ds(r, TILE), lanes],
                        key[k, :, lanes],
                        (((1,), (1,)), ((), ())),
                        preferred_element_type=jnp.float32,
                    )
                    seen = col >= lowest - meta[k]
                    if k == 0:
                        seen = seen & (col <= row + r)
                    scores.append(jnp.where(seen, part, NEG_FILL))
                top = scores[0]
                for part in scores[1:]:
                    top = jnp.maximum(top, part)
                top = jnp.max(top, axis=1, keepdims=True)
                acc = None
                for k in range(count):
                    weights = jnp.exp(scores[k] - top).astype(jnp.bfloat16)
                    value = jnp.concatenate([pieces[k][:, lanes], ones], axis=1)
                    product = jnp.dot(weights, value, preferred_element_type=jnp.float32)
                    acc = product if acc is None else acc + product
                out = (acc[:, :HD] / acc[:, HD:]).astype(jnp.bfloat16)
                mixed[(h % 2 + odd) % 2, pl.ds(r, TILE), (h // 2) * HD : (h // 2 + 1) * HD] = out
            return carry

        lax.fori_loop(0, rows // TILE, tile, 0)

    for count in range(1, 6):

        @pl.when(meta[5] == count)
        def _(count=count):
            attend(count)

    keep[...] = mixed[0]
    give[...] = mixed[1]
    pack[...] = mixed[0, rows - pack.shape[0] :]


def attention(meta, pieces, low, q_gain, k_gain, below):
    rows, width = pieces[0].shape
    lanes = GROUP * HD
    by_group = pl.BlockSpec((rows, lanes), lambda g, meta: (0, g))
    gain = pl.BlockSpec((1, lanes), lambda g, meta: (0, g))
    return pl.pallas_call(
        attention_body,
        grid_spec=pltpu.PrefetchScalarGridSpec(
            num_scalar_prefetch=1,
            grid=(width // lanes,),
            in_specs=[by_group] * 5 + [pl.BlockSpec((rows, HD), lambda g, meta: (0, 0)), gain, gain],
            out_specs=[pl.BlockSpec((rows, lanes // 2), lambda g, meta: (0, g))] * 2
            + [pl.BlockSpec((below, lanes // 2), lambda g, meta: (0, g))],
            scratch_shapes=[pltpu.VMEM((2, rows, lanes // 2), jnp.bfloat16)]
            + [pltpu.VMEM((rows, lanes), jnp.bfloat16)] * 3
            + [pltpu.VMEM((5, rows, lanes), jnp.bfloat16)],
        ),
        out_shape=[jax.ShapeDtypeStruct((count, width // 2), jnp.bfloat16) for count in (rows, rows, 2 * below)],
        cost_estimate=pl.CostEstimate(
            flops=2 * 5 * rows * rows * width, bytes_accessed=12 * rows * width, transcendentals=5 * rows * rows * width // HD
        ),
        name="attention",
    )(meta, *pieces, low, q_gain, k_gain)


def stage_body(*refs):
    weights, staged, sems = refs[:16], refs[16], refs[17]
    depth = weights[0].shape[0]
    copies = [
        pltpu.make_async_copy(weights[k], staged.at[pl.ds(k * depth, depth)], sems.at[k]) for k in range(len(weights))
    ]
    for copy in copies:
        copy.start()
    for copy in copies:
        copy.wait()


def stage(weights):
    depth, width = weights[0].shape
    count = len(weights)
    return pl.pallas_call(
        stage_body,
        in_specs=[pl.BlockSpec(memory_space=pl.ANY)] * count,
        out_specs=pl.BlockSpec(memory_space=pltpu.VMEM),
        out_shape=jax.ShapeDtypeStruct((count * depth, width), jnp.bfloat16),
        scratch_shapes=[pltpu.SemaphoreType.DMA((count,))],
        compiler_params=pltpu.CompilerParams(vmem_limit_bytes=4 << 20),
        cost_estimate=pl.CostEstimate(flops=0, bytes_accessed=4 * count * depth * width, transcendentals=0),
        name="stage",
    )(*weights)


def arrange(meta, parts, left):
    sides = len(parts) // 4
    n_rows, lanes = parts[0].shape
    depth = lanes // 4
    z, tensor, y_low = meta[0], meta[1], meta[2]
    for rel, shift in enumerate((0, 1, 3, 2)):
        for zz in range(2):
            slot = (z - (2 * ((tensor + 4 - shift) % 4) + zz) + 8) % 8
            for side in range(sides):
                ref = parts[sides * rel + side]
                rows = slice(side * n_rows, (side + 1) * n_rows)

                @pl.when(y_low == 0)
                def _(slot=slot, ref=ref, rows=rows, zz=zz):
                    left[slot, rows] = ref[:, 2 * zz * depth : (2 * zz + 2) * depth]

                @pl.when(y_low != 0)
                def _(slot=slot, ref=ref, rows=rows, zz=zz):
                    left[slot, rows, 0:depth] = ref[:, (2 * zz + 1) * depth : (2 * zz + 2) * depth]
                    left[slot, rows, depth : 2 * depth] = ref[:, 2 * zz * depth : (2 * zz + 1) * depth]


def multiply(left, staged, own, other, begin):
    n_rows, width = own.shape

    def chunk(c, carry):
        at = pl.multiple_of(c * CHUNK, CHUNK)
        whole = jnp.concatenate([left[k] for k in range(8)], axis=1)
        total = jnp.dot(whole, staged[:, pl.ds(begin + at, CHUNK)], preferred_element_type=jnp.float32)
        own[:, pl.ds(at, CHUNK)] = total[:n_rows]
        other[:, pl.ds(at, CHUNK)] = total[n_rows:]
        return carry

    lax.fori_loop(0, width // CHUNK, chunk, 0)


def first_body(meta, *refs):
    parts, (staged, own, other, left) = refs[:-4], refs[-4:]
    arrange(meta, parts, left)
    multiply(left, staged, own, other, 0)


def later_body(left, staged, own, other, begin):
    multiply(left, staged, own, other, begin)


def project(meta, parts, staged, width, begin=0, left=None):
    rows = parts[0].shape[0] * len(parts) // 8
    lanes = parts[0].shape[1]
    depth = staged.shape[0]
    vmem = pl.BlockSpec(memory_space=pltpu.VMEM)
    result = jax.ShapeDtypeStruct((rows, width), jnp.float32)
    options = dict(
        compiler_params=pltpu.CompilerParams(vmem_limit_bytes=12 << 20),
        cost_estimate=pl.CostEstimate(
            flops=4 * rows * depth * width, bytes_accessed=2 * depth * width, transcendentals=0
        ),
        name="project",
    )
    if left is None:
        return pl.pallas_call(
            first_body,
            in_specs=[pl.BlockSpec(memory_space=pltpu.SMEM)] + [vmem] * (len(parts) + 1),
            out_specs=[vmem] * 3,
            out_shape=[result, result, jax.ShapeDtypeStruct((8, 2 * rows, lanes // 2), jnp.bfloat16)],
            **options,
        )(meta, *parts, staged)
    return pl.pallas_call(
        functools.partial(later_body, begin=begin),
        in_specs=[vmem] * 2,
        out_specs=[vmem] * 2,
        out_shape=[result, result],
        **options,
    )(left, staged)


def per_device(resid, streams, filt, q_gain, k_gain, out_weight, contig_lengths):
    resid_own = resid[0]
    streams_own = jnp.transpose(streams[0], (0, 2, 1, 3))
    rows = resid_own.shape[1]
    section = lax.axis_index("pipe")
    seq = lax.axis_index("seq")
    tensor = lax.axis_index("tensor")
    n_seq = lax.axis_size("seq")
    n_tensor = lax.axis_size("tensor")
    n_z = n_seq // 4
    core = seq % 2
    y_low = (seq // 2) % 2
    both = ("pipe", "seq")

    def along_y(value, step):
        pairs = []
        for y in range(4):
            to = (y + step) % 4
            for z in range(n_z):
                for c in range(2):
                    pairs.append(((y // 2) * n_seq + z * 4 + (y % 2) * 2 + c, (to // 2) * n_seq + z * 4 + (to % 2) * 2 + c))
        return lax.ppermute(value, both, pairs)

    def along_z(value, step):
        return lax.ppermute(value, "seq", [(s, (s + 4 * step) % n_seq) for s in range(n_seq)])

    def along_tensor(value, step):
        return lax.ppermute(value, "tensor", [(t, (t + step) % n_tensor) for t in range(n_tensor)])

    partner = [(s, s ^ 1) for s in range(n_seq)]
    tail = tail_of(streams_own)
    prev = lax.ppermute(tail, "seq", [(s, s + 1) for s in range(n_seq - 1)])
    output, attend_1 = hyena(streams_own, resid_own, prev, filt, 1)
    arrived = lax.ppermute(attend_1, "pipe", [(0, 1)])
    output, attend_0 = hyena(streams_own, resid_own, prev, filt, 0, output)

    right, left = [out_weight], [out_weight]
    across = {0: along_y(out_weight, 1)}
    for k in range(1, 5):
        right.append(along_z(right[-1], 1))
        across[k] = along_y(right[k], 1 if k < 4 else -1)
        if k < 4:
            left.append(along_z(left[-1], -1))
            across[8 - k] = along_y(left[k], -1)
    same = right + [left[k] for k in (3, 2, 1)]
    weights = []
    for k in range(8):
        weights += [same[k], across[k]]

    own = jnp.where(section == 0, attend_0, arrived)
    behind = lax.ppermute(own, "seq", [(s, s + 4) for s in range(n_seq - 4)])
    mid = lax.ppermute(jnp.where(y_low == 0, own, behind), "seq", [(s, s ^ 2) for s in range(n_seq)])
    beside = lax.ppermute(jnp.where(core == 0, own, behind), "seq", partner)
    beside_2 = lax.ppermute(mid, "seq", partner)
    pieces = (own, behind, mid, beside, beside_2)

    contig_ends = jnp.cumsum(contig_lengths, axis=1)[section]
    start = seq * rows
    query_pos = start + jnp.arange(rows, dtype=jnp.int32)
    low = jnp.max(jnp.where(contig_ends[None, :] <= query_pos[:, None], contig_ends[None, :], 0), axis=1)
    first_low = jnp.max(jnp.where(contig_ends <= start, contig_ends, 0))
    count = 1 + (start - first_low + rows - 1) // rows
    slots = jnp.arange(8, dtype=jnp.int32)
    split = rows * 3 // 8
    meta = jnp.where(slots < 5, start - rows * slots, jnp.where(slots == 5, count, core))
    low = jnp.broadcast_to(low[:, None], (rows, HD)).astype(jnp.int32)
    keep, give, pack = attention(
        meta, pieces, low, q_gain[None, :] * (1.0 / HD), k_gain[None, :], rows - split
    )

    got = lax.ppermute(give, "seq", partner)
    keep_1, keep_3 = along_tensor(keep, 1), along_tensor(keep, -1)
    got_1, got_3 = along_tensor(got, 1), along_tensor(got, -1)
    pack = lax.dynamic_update_slice(pack, got[split:], (rows - split, 0))
    below = lax.ppermute(pack, "pipe", [(0, 1)])
    keep_2, got_2 = along_tensor(keep_1, 1), along_tensor(got_3, -1)
    parts = [keep, got, keep_1, got_1, keep_3, got_3, keep_2, got_2]
    below_parts = [below] + [along_tensor(below, step) for step in (1, -1, 2)]
    place = jnp.where(slots == 0, seq // 4, jnp.where(slots == 1, tensor, y_low))

    def put(output, batch, row, col, value):
        at = (batch, row, col)
        old = lax.dynamic_slice(output, at, (1,) + value.shape)
        return lax.dynamic_update_slice(output, jnp.where(section == 0, old, value[None]), at)

    staged = stage(weights)
    width = staged.shape[1] // HALVES
    returned, lhs = [], None
    for half in range(HALVES):
        own, other, *rest = project(place, parts, staged, width, half * width, lhs)
        lhs = rest[0] if rest else lhs
        other = lax.ppermute(other, "seq", partner)
        part = (own + other).astype(jnp.bfloat16)
        returned.append(lax.ppermute(part[:split], "pipe", [(0, 1)]))
        output = put(output, 1, 0, half * width, part)
    own, other, _ = project(place, below_parts, staged, staged.shape[1])
    other = lax.ppermute(other, "seq", partner)
    output = put(output, 0, split, 0, (own + other).astype(jnp.bfloat16))
    for half in range(HALVES):
        output = put(output, 0, 0, half * width, returned[half])
    return output[None]


def solution(mesh):
    placed = (
        P("pipe", None, "seq", "tensor"),
        P("pipe", None, "seq", None, "tensor"),
        P(None, "tensor"),
        P("tensor"),
        P("tensor"),
        P("seq", "tensor"),
        P(),
    )
    return jax.shard_map(
        per_device,
        mesh=mesh,
        in_specs=placed,
        out_specs=P("pipe", None, "seq", "tensor"),
        check_vma=False,
    )
```

```python
import functools

import jax
import jax.numpy as jnp
from jax import lax
from jax.experimental import pallas as pl
from jax.experimental.pallas import tpu as pltpu
from jax.sharding import PartitionSpec as P


HD = 128
NEG_FILL = -1e30
HALO = 8
COLS = 512
ROWS = 32
TILE = 128
GROUP = 4


HALVES = 2
CHUNK = 512


def tail_body(stream, tail):
    for b in range(stream.shape[0]):
        gate = stream[b, 0].astype(jnp.float32) * stream[b, 2].astype(jnp.float32)
        tail[b] = gate.astype(jnp.bfloat16)


def tail_of(streams):
    batches, kinds, rows, width = streams.shape
    return pl.pallas_call(
        tail_body,
        grid=(1,),
        in_specs=[pl.BlockSpec((batches, kinds, HALO, width), lambda i: (0, 0, rows // HALO - 1, 0))],
        out_specs=pl.BlockSpec((batches, HALO, width), lambda i: (0, 0, 0)),
        out_shape=jax.ShapeDtypeStruct((batches, HALO, width), jnp.bfloat16),
        name="tail",
    )(streams)


def hyena_body(stream, resid, prev, filt, *rest):
    hidden, attend, extended = rest[-3:]
    taps = filt.shape[0]
    rows, cols = resid.shape
    extended[0:HALO] = prev[...].astype(jnp.float32)
    for r in range(0, rows, ROWS):
        gate = stream[0, r : r + ROWS].astype(jnp.float32) * stream[2, r : r + ROWS].astype(jnp.float32)
        extended[HALO + r : HALO + r + ROWS] = gate.astype(jnp.bfloat16).astype(jnp.float32)
    weights = [filt[j : j + 1].astype(jnp.float32) for j in range(taps)]
    for r in range(0, rows, ROWS):
        conv = weights[0] * extended[HALO + r : HALO + r + ROWS]
        for j in range(1, taps):
            conv = conv + weights[j] * extended[HALO + r - j : HALO + r - j + ROWS]
        mixed = resid[r : r + ROWS].astype(jnp.float32) + stream[1, r : r + ROWS].astype(jnp.float32) * conv
        mixed = mixed.astype(jnp.bfloat16)
        hidden[r : r + ROWS] = mixed
        for c in range(cols // (2 * HD)):
            attend[r : r + ROWS, c * HD : (c + 1) * HD] = mixed[:, 2 * c * HD : (2 * c + 1) * HD]


def hyena(streams, resid, prev, filt, batch, into=None):
    batches, _, rows, width = streams.shape
    taps = filt.shape[0]
    extra = [] if into is None else [into]
    return pl.pallas_call(
        hyena_body,
        grid=(width // COLS,),
        in_specs=[
            pl.BlockSpec((None, 3, rows, COLS), lambda c: (batch, 0, 0, c)),
            pl.BlockSpec((None, rows, COLS), lambda c: (batch, 0, c)),
            pl.BlockSpec((None, HALO, COLS), lambda c: (batch, 0, c)),
            pl.BlockSpec((taps, COLS), lambda c: (0, c)),
        ]
        + [pl.BlockSpec(memory_space=pl.ANY)] * len(extra),
        out_specs=[
            pl.BlockSpec((None, rows, COLS), lambda c: (batch, 0, c)),
            pl.BlockSpec((rows, COLS // 2), lambda c: (0, c)),
        ],
        out_shape=[
            jax.ShapeDtypeStruct((batches, rows, width), jnp.bfloat16),
            jax.ShapeDtypeStruct((rows, width // 2), jnp.bfloat16),
        ],
        scratch_shapes=[pltpu.VMEM((HALO + rows, COLS), jnp.float32)],
        input_output_aliases={4: 0} if extra else {},
        cost_estimate=pl.CostEstimate(flops=20 * rows * width, bytes_accessed=11 * rows * width, transcendentals=0),
        name="hyena",
    )(streams, resid, prev, filt, *extra)


def attention_body(meta, *refs):
    own, far, mid, side_a, side_b, low, q_gain, k_gain, keep, give, pack, mixed, near, third, query, key = refs
    rows, _ = own.shape
    odd = meta[6]

    @pl.when(odd == 0)
    def _():
        near[...] = side_b[...]
        third[...] = side_a[...]

    @pl.when(odd != 0)
    def _():
        near[...] = side_a[...]
        third[...] = side_b[...]

    pieces = (own, near, mid, third, far)
    ones = jnp.ones((rows, HD), jnp.bfloat16)
    col = lax.broadcasted_iota(jnp.int32, (TILE, rows), 1)
    row = lax.broadcasted_iota(jnp.int32, (TILE, rows), 0)

    def attend(count):
        for h in range(GROUP):
            lanes = slice(h * HD, (h + 1) * HD)
            query[:, lanes] = (own[:, lanes].astype(jnp.float32) * q_gain[:, lanes]).astype(jnp.bfloat16)
            for k, ref in enumerate(pieces[:count]):
                key[k, :, lanes] = (ref[:, lanes].astype(jnp.float32) * k_gain[:, lanes]).astype(jnp.bfloat16)

        def tile(t, carry):
            r = pl.multiple_of(t * TILE, TILE)
            lowest = low[pl.ds(r, TILE)]
            lowest = jnp.concatenate([lowest] * (rows // HD), axis=1)
            for h in range(GROUP):
                lanes = slice(h * HD, (h + 1) * HD)
                scores = []
                for k in range(count):
                    part = lax.dot_general(
                        query[pl.ds(r, TILE), lanes],
                        key[k, :, lanes],
                        (((1,), (1,)), ((), ())),
                        preferred_element_type=jnp.float32,
                    )
                    seen = col >= lowest - meta[k]
                    if k == 0:
                        seen = seen & (col <= row + r)
                    scores.append(jnp.where(seen, part, NEG_FILL))
                top = scores[0]
                for part in scores[1:]:
                    top = jnp.maximum(top, part)
                top = jnp.max(top, axis=1, keepdims=True)
                acc = None
                for k in range(count):
                    weights = jnp.exp(scores[k] - top).astype(jnp.bfloat16)
                    value = jnp.concatenate([pieces[k][:, lanes], ones], axis=1)
                    product = jnp.dot(weights, value, preferred_element_type=jnp.float32)
                    acc = product if acc is None else acc + product
                out = (acc[:, :HD] / acc[:, HD:]).astype(jnp.bfloat16)
                mixed[(h % 2 + odd) % 2, pl.ds(r, TILE), (h // 2) * HD : (h // 2 + 1) * HD] = out
            return carry

        lax.fori_loop(0, rows // TILE, tile, 0)

    for count in range(1, 6):

        @pl.when(meta[5] == count)
        def _(count=count):
            attend(count)

    keep[...] = mixed[0]
    give[...] = mixed[1]
    pack[...] = mixed[0, rows - pack.shape[0] :]


def attention(meta, pieces, low, q_gain, k_gain, below):
    rows, width = pieces[0].shape
    lanes = GROUP * HD
    by_group = pl.BlockSpec((rows, lanes), lambda g, meta: (0, g))
    gain = pl.BlockSpec((1, lanes), lambda g, meta: (0, g))
    return pl.pallas_call(
        attention_body,
        grid_spec=pltpu.PrefetchScalarGridSpec(
            num_scalar_prefetch=1,
            grid=(width // lanes,),
            in_specs=[by_group] * 5 + [pl.BlockSpec((rows, HD), lambda g, meta: (0, 0)), gain, gain],
            out_specs=[pl.BlockSpec((rows, lanes // 2), lambda g, meta: (0, g))] * 2
            + [pl.BlockSpec((below, lanes // 2), lambda g, meta: (0, g))],
            scratch_shapes=[pltpu.VMEM((2, rows, lanes // 2), jnp.bfloat16)]
            + [pltpu.VMEM((rows, lanes), jnp.bfloat16)] * 3
            + [pltpu.VMEM((5, rows, lanes), jnp.bfloat16)],
        ),
        out_shape=[jax.ShapeDtypeStruct((count, width // 2), jnp.bfloat16) for count in (rows, rows, 2 * below)],
        cost_estimate=pl.CostEstimate(
            flops=2 * 5 * rows * rows * width, bytes_accessed=12 * rows * width, transcendentals=5 * rows * rows * width // HD
        ),
        name="attention",
    )(meta, *pieces, low, q_gain, k_gain)


def stage_body(*refs):
    weights, staged, sems = refs[:16], refs[16], refs[17]
    depth = weights[0].shape[0]
    copies = [
        pltpu.make_async_copy(weights[k], staged.at[pl.ds(k * depth, depth)], sems.at[k]) for k in range(len(weights))
    ]
    for copy in copies:
        copy.start()
    for copy in copies:
        copy.wait()


def stage(weights):
    depth, width = weights[0].shape
    count = len(weights)
    return pl.pallas_call(
        stage_body,
        in_specs=[pl.BlockSpec(memory_space=pl.ANY)] * count,
        out_specs=pl.BlockSpec(memory_space=pltpu.VMEM),
        out_shape=jax.ShapeDtypeStruct((count * depth, width), jnp.bfloat16),
        scratch_shapes=[pltpu.SemaphoreType.DMA((count,))],
        compiler_params=pltpu.CompilerParams(vmem_limit_bytes=4 << 20),
        cost_estimate=pl.CostEstimate(flops=0, bytes_accessed=4 * count * depth * width, transcendentals=0),
        name="stage",
    )(*weights)


def arrange(meta, parts, left):
    sides = len(parts) // 4
    n_rows, lanes = parts[0].shape
    depth = lanes // 4
    z, tensor, y_low = meta[0], meta[1], meta[2]
    for rel, shift in enumerate((0, 1, 3, 2)):
        for zz in range(2):
            slot = (z - (2 * ((tensor + 4 - shift) % 4) + zz) + 8) % 8
            for side in range(sides):
                ref = parts[sides * rel + side]
                rows = slice(side * n_rows, (side + 1) * n_rows)

                @pl.when(y_low == 0)
                def _(slot=slot, ref=ref, rows=rows, zz=zz):
                    left[slot, rows] = ref[:, 2 * zz * depth : (2 * zz + 2) * depth]

                @pl.when(y_low != 0)
                def _(slot=slot, ref=ref, rows=rows, zz=zz):
                    left[slot, rows, 0:depth] = ref[:, (2 * zz + 1) * depth : (2 * zz + 2) * depth]
                    left[slot, rows, depth : 2 * depth] = ref[:, 2 * zz * depth : (2 * zz + 1) * depth]


def multiply(left, staged, own, other, begin):
    n_rows, width = own.shape

    def chunk(c, carry):
        at = pl.multiple_of(c * CHUNK, CHUNK)
        whole = jnp.concatenate([left[k] for k in range(8)], axis=1)
        total = jnp.dot(whole, staged[:, pl.ds(begin + at, CHUNK)], preferred_element_type=jnp.float32)
        own[:, pl.ds(at, CHUNK)] = total[:n_rows]
        other[:, pl.ds(at, CHUNK)] = total[n_rows:]
        return carry

    lax.fori_loop(0, width // CHUNK, chunk, 0)


def first_body(meta, *refs):
    parts, (staged, own, other, left) = refs[:-4], refs[-4:]
    arrange(meta, parts, left)
    multiply(left, staged, own, other, 0)


def later_body(left, staged, own, other, begin):
    multiply(left, staged, own, other, begin)


def project(meta, parts, staged, width, begin=0, left=None):
    rows = parts[0].shape[0] * len(parts) // 8
    lanes = parts[0].shape[1]
    depth = staged.shape[0]
    vmem = pl.BlockSpec(memory_space=pltpu.VMEM)
    result = jax.ShapeDtypeStruct((rows, width), jnp.float32)
    options = dict(
        compiler_params=pltpu.CompilerParams(vmem_limit_bytes=12 << 20),
        cost_estimate=pl.CostEstimate(
            flops=4 * rows * depth * width, bytes_accessed=2 * depth * width, transcendentals=0
        ),
        name="project",
    )
    if left is None:
        return pl.pallas_call(
            first_body,
            in_specs=[pl.BlockSpec(memory_space=pltpu.SMEM)] + [vmem] * (len(parts) + 1),
            out_specs=[vmem] * 3,
            out_shape=[result, result, jax.ShapeDtypeStruct((8, 2 * rows, lanes // 2), jnp.bfloat16)],
            **options,
        )(meta, *parts, staged)
    return pl.pallas_call(
        functools.partial(later_body, begin=begin),
        in_specs=[vmem] * 2,
        out_specs=[vmem] * 2,
        out_shape=[result, result],
        **options,
    )(left, staged)


def per_device(resid, streams, filt, q_gain, k_gain, out_weight, contig_lengths):
    resid_own = resid[0]
    streams_own = jnp.transpose(streams[0], (0, 2, 1, 3))
    rows = resid_own.shape[1]
    section = lax.axis_index("pipe")
    seq = lax.axis_index("seq")
    tensor = lax.axis_index("tensor")
    n_seq = lax.axis_size("seq")
    n_tensor = lax.axis_size("tensor")
    n_z = n_seq // 4
    core = seq % 2
    y_low = (seq // 2) % 2
    both = ("pipe", "seq")

    def along_y(value, step):
        pairs = []
        for y in range(4):
            to = (y + step) % 4
            for z in range(n_z):
                for c in range(2):
                    pairs.append(((y // 2) * n_seq + z * 4 + (y % 2) * 2 + c, (to // 2) * n_seq + z * 4 + (to % 2) * 2 + c))
        return lax.ppermute(value, both, pairs)

    def along_z(value, step):
        return lax.ppermute(value, "seq", [(s, (s + 4 * step) % n_seq) for s in range(n_seq)])

    def along_tensor(value, step):
        return lax.ppermute(value, "tensor", [(t, (t + step) % n_tensor) for t in range(n_tensor)])

    partner = [(s, s ^ 1) for s in range(n_seq)]
    tail = tail_of(streams_own)
    prev = lax.ppermute(tail, "seq", [(s, s + 1) for s in range(n_seq - 1)])
    output, attend_1 = hyena(streams_own, resid_own, prev, filt, 1)
    arrived = lax.ppermute(attend_1, "pipe", [(0, 1)])
    output, attend_0 = hyena(streams_own, resid_own, prev, filt, 0, output)

    right, left = [out_weight], [out_weight]
    across = {0: along_y(out_weight, 1)}
    for k in range(1, 5):
        right.append(along_z(right[-1], 1))
        across[k] = along_y(right[k], 1 if k < 4 else -1)
        if k < 4:
            left.append(along_z(left[-1], -1))
            across[8 - k] = along_y(left[k], -1)
    same = right + [left[k] for k in (3, 2, 1)]
    weights = []
    for k in range(8):
        weights += [same[k], across[k]]

    contig_ends = jnp.cumsum(contig_lengths, axis=1)[section]
    start = seq * rows
    query_pos = start + jnp.arange(rows, dtype=jnp.int32)
    low = jnp.max(jnp.where(contig_ends[None, :] <= query_pos[:, None], contig_ends[None, :], 0), axis=1)
    first_low = jnp.max(jnp.where(contig_ends <= start, contig_ends, 0))
    count = 1 + (start - first_low + rows - 1) // rows
    slots = jnp.arange(8, dtype=jnp.int32)
    split = rows * 7 // 16
    meta = jnp.where(slots < 5, start - rows * slots, jnp.where(slots == 5, count, core))
    low = jnp.broadcast_to(low[:, None], (rows, HD)).astype(jnp.int32)
    gain = q_gain[None, :] * (1.0 / HD)
    attend_0, meta, low, gain = lax.optimization_barrier((attend_0, meta, low, gain))
    own = jnp.where(section == 0, attend_0, arrived)
    behind = lax.ppermute(own, "seq", [(s, s + 4) for s in range(n_seq - 4)])
    mid = lax.ppermute(jnp.where(y_low == 0, own, behind), "seq", [(s, s ^ 2) for s in range(n_seq)])
    beside = lax.ppermute(jnp.where(core == 0, own, behind), "seq", partner)
    beside_2 = lax.ppermute(mid, "seq", partner)
    pieces = (own, behind, mid, beside, beside_2)

    keep, give, pack = attention(
        meta, pieces, low, gain, k_gain[None, :], rows - split
    )

    got = lax.ppermute(give, "seq", partner)
    keep_1, keep_3 = along_tensor(keep, 1), along_tensor(keep, -1)
    got_1, got_3 = along_tensor(got, 1), along_tensor(got, -1)
    pack = lax.dynamic_update_slice(pack, got[split:], (rows - split, 0))
    below = lax.ppermute(pack, "pipe", [(0, 1)])
    keep_2, got_2 = along_tensor(keep_1, 1), along_tensor(got_3, -1)
    parts = [keep, got, keep_1, got_1, keep_3, got_3, keep_2, got_2]
    below_parts = [below] + [along_tensor(below, step) for step in (1, -1, 2)]
    place = jnp.where(slots == 0, seq // 4, jnp.where(slots == 1, tensor, y_low))

    def put(output, batch, row, col, value):
        at = (batch, row, col)
        old = lax.dynamic_slice(output, at, (1,) + value.shape)
        return lax.dynamic_update_slice(output, jnp.where(section == 0, old, value[None]), at)

    staged = stage(weights)
    width = staged.shape[1] // HALVES
    returned, lhs = [], None
    for half in range(HALVES):
        own, other, *rest = project(place, parts, staged, width, half * width, lhs)
        lhs = rest[0] if rest else lhs
        other = lax.ppermute(other, "seq", partner)
        part = (own + other).astype(jnp.bfloat16)
        returned.append(lax.ppermute(part[:split], "pipe", [(0, 1)]))
        output = put(output, 1, 0, half * width, part)
    own, other, _ = project(place, below_parts, staged, staged.shape[1])
    other = lax.ppermute(other, "seq", partner)
    output = put(output, 0, split, 0, (own + other).astype(jnp.bfloat16))
    for half in range(HALVES):
        output = put(output, 0, 0, half * width, returned[half])
    return output[None]


def solution(mesh):
    placed = (
        P("pipe", None, "seq", "tensor"),
        P("pipe", None, "seq", None, "tensor"),
        P(None, "tensor"),
        P("tensor"),
        P("tensor"),
        P("seq", "tensor"),
        P(),
    )
    return jax.shard_map(
        per_device,
        mesh=mesh,
        in_specs=placed,
        out_specs=P("pipe", None, "seq", "tensor"),
        check_vma=False,
    )
```

```python
import functools

import jax
import jax.numpy as jnp
from jax import lax
from jax.experimental import pallas as pl
from jax.experimental.pallas import tpu as pltpu
from jax.sharding import PartitionSpec as P


HD = 128
NEG_FILL = -1e30
HALO = 8
COLS = 512
ROWS = 32
TILE = 128
GROUP = 4


HALVES = 2
CHUNK = 512


def tail_body(stream, tail):
    for b in range(stream.shape[0]):
        gate = stream[b, 0].astype(jnp.float32) * stream[b, 2].astype(jnp.float32)
        tail[b] = gate.astype(jnp.bfloat16)


def tail_of(streams):
    batches, kinds, rows, width = streams.shape
    return pl.pallas_call(
        tail_body,
        grid=(1,),
        in_specs=[pl.BlockSpec((batches, kinds, HALO, width), lambda i: (0, 0, rows // HALO - 1, 0))],
        out_specs=pl.BlockSpec((batches, HALO, width), lambda i: (0, 0, 0)),
        out_shape=jax.ShapeDtypeStruct((batches, HALO, width), jnp.bfloat16),
        name="tail",
    )(streams)


def hyena_body(stream, resid, prev, filt, *rest):
    hidden, attend, extended = rest[-3:]
    taps = filt.shape[0]
    rows, cols = resid.shape
    extended[0:HALO] = prev[...].astype(jnp.float32)
    for r in range(0, rows, ROWS):
        gate = stream[0, r : r + ROWS].astype(jnp.float32) * stream[2, r : r + ROWS].astype(jnp.float32)
        extended[HALO + r : HALO + r + ROWS] = gate.astype(jnp.bfloat16).astype(jnp.float32)
    weights = [filt[j : j + 1].astype(jnp.float32) for j in range(taps)]
    for r in range(0, rows, ROWS):
        conv = weights[0] * extended[HALO + r : HALO + r + ROWS]
        for j in range(1, taps):
            conv = conv + weights[j] * extended[HALO + r - j : HALO + r - j + ROWS]
        mixed = resid[r : r + ROWS].astype(jnp.float32) + stream[1, r : r + ROWS].astype(jnp.float32) * conv
        mixed = mixed.astype(jnp.bfloat16)
        hidden[r : r + ROWS] = mixed
        for c in range(cols // (2 * HD)):
            attend[r : r + ROWS, c * HD : (c + 1) * HD] = mixed[:, 2 * c * HD : (2 * c + 1) * HD]


def hyena(streams, resid, prev, filt, batch, into=None):
    batches, _, rows, width = streams.shape
    taps = filt.shape[0]
    extra = [] if into is None else [into]
    return pl.pallas_call(
        hyena_body,
        grid=(width // COLS,),
        in_specs=[
            pl.BlockSpec((None, 3, rows, COLS), lambda c: (batch, 0, 0, c)),
            pl.BlockSpec((None, rows, COLS), lambda c: (batch, 0, c)),
            pl.BlockSpec((None, HALO, COLS), lambda c: (batch, 0, c)),
            pl.BlockSpec((taps, COLS), lambda c: (0, c)),
        ]
        + [pl.BlockSpec(memory_space=pl.ANY)] * len(extra),
        out_specs=[
            pl.BlockSpec((None, rows, COLS), lambda c: (batch, 0, c)),
            pl.BlockSpec((rows, COLS // 2), lambda c: (0, c)),
        ],
        out_shape=[
            jax.ShapeDtypeStruct((batches, rows, width), jnp.bfloat16),
            jax.ShapeDtypeStruct((rows, width // 2), jnp.bfloat16),
        ],
        scratch_shapes=[pltpu.VMEM((HALO + rows, COLS), jnp.float32)],
        input_output_aliases={4: 0} if extra else {},
        cost_estimate=pl.CostEstimate(flops=20 * rows * width, bytes_accessed=11 * rows * width, transcendentals=0),
        name="hyena",
    )(streams, resid, prev, filt, *extra)


def attention_body(meta, *refs):
    own, far, mid, side_a, side_b, low, q_gain, k_gain, keep, give, pack, mixed, near, third, query, key = refs
    rows, _ = own.shape
    odd = meta[6]

    @pl.when(odd == 0)
    def _():
        near[...] = side_b[...]
        third[...] = side_a[...]

    @pl.when(odd != 0)
    def _():
        near[...] = side_a[...]
        third[...] = side_b[...]

    pieces = (own, near, mid, third, far)
    ones = jnp.ones((rows, HD), jnp.bfloat16)
    col = lax.broadcasted_iota(jnp.int32, (TILE, rows), 1)
    row = lax.broadcasted_iota(jnp.int32, (TILE, rows), 0)

    def attend(count):
        for h in range(GROUP):
            lanes = slice(h * HD, (h + 1) * HD)
            query[:, lanes] = (own[:, lanes].astype(jnp.float32) * q_gain[:, lanes]).astype(jnp.bfloat16)
            for k, ref in enumerate(pieces[:count]):
                key[k, :, lanes] = (ref[:, lanes].astype(jnp.float32) * k_gain[:, lanes]).astype(jnp.bfloat16)

        def tile(t, carry):
            r = pl.multiple_of(t * TILE, TILE)
            lowest = low[pl.ds(r, TILE)]
            lowest = jnp.concatenate([lowest] * (rows // HD), axis=1)
            for h in range(GROUP):
                lanes = slice(h * HD, (h + 1) * HD)
                scores = []
                for k in range(count):
                    part = lax.dot_general(
                        query[pl.ds(r, TILE), lanes],
                        key[k, :, lanes],
                        (((1,), (1,)), ((), ())),
                        preferred_element_type=jnp.float32,
                    )
                    seen = col >= lowest - meta[k]
                    if k == 0:
                        seen = seen & (col <= row + r)
                    scores.append(jnp.where(seen, part, NEG_FILL))
                top = scores[0]
                for part in scores[1:]:
                    top = jnp.maximum(top, part)
                top = jnp.max(top, axis=1, keepdims=True)
                acc = None
                for k in range(count):
                    weights = jnp.exp(scores[k] - top).astype(jnp.bfloat16)
                    value = jnp.concatenate([pieces[k][:, lanes], ones], axis=1)
                    product = jnp.dot(weights, value, preferred_element_type=jnp.float32)
                    acc = product if acc is None else acc + product
                out = (acc[:, :HD] / acc[:, HD:]).astype(jnp.bfloat16)
                mixed[(h % 2 + odd) % 2, pl.ds(r, TILE), (h // 2) * HD : (h // 2 + 1) * HD] = out
            return carry

        lax.fori_loop(0, rows // TILE, tile, 0)

    for count in range(1, 6):

        @pl.when(meta[5] == count)
        def _(count=count):
            attend(count)

    keep[...] = mixed[0]
    give[...] = mixed[1]
    pack[...] = mixed[0, rows - pack.shape[0] :]


def attention(meta, pieces, low, q_gain, k_gain, below):
    rows, width = pieces[0].shape
    lanes = GROUP * HD
    by_group = pl.BlockSpec((rows, lanes), lambda g, meta: (0, g))
    gain = pl.BlockSpec((1, lanes), lambda g, meta: (0, g))
    return pl.pallas_call(
        attention_body,
        grid_spec=pltpu.PrefetchScalarGridSpec(
            num_scalar_prefetch=1,
            grid=(width // lanes,),
            in_specs=[by_group] * 5 + [pl.BlockSpec((rows, HD), lambda g, meta: (0, 0)), gain, gain],
            out_specs=[pl.BlockSpec((rows, lanes // 2), lambda g, meta: (0, g))] * 2
            + [pl.BlockSpec((below, lanes // 2), lambda g, meta: (0, g))],
            scratch_shapes=[pltpu.VMEM((2, rows, lanes // 2), jnp.bfloat16)]
            + [pltpu.VMEM((rows, lanes), jnp.bfloat16)] * 3
            + [pltpu.VMEM((5, rows, lanes), jnp.bfloat16)],
        ),
        out_shape=[jax.ShapeDtypeStruct((count, width // 2), jnp.bfloat16) for count in (rows, rows, 2 * below)],
        cost_estimate=pl.CostEstimate(
            flops=2 * 5 * rows * rows * width, bytes_accessed=12 * rows * width, transcendentals=5 * rows * rows * width // HD
        ),
        name="attention",
    )(meta, *pieces, low, q_gain, k_gain)


def stage_body(*refs):
    weights, staged, sems = refs[:16], refs[16], refs[17]
    depth = weights[0].shape[0]
    copies = [
        pltpu.make_async_copy(weights[k], staged.at[pl.ds(k * depth, depth)], sems.at[k]) for k in range(len(weights))
    ]
    for copy in copies:
        copy.start()
    for copy in copies:
        copy.wait()


def stage(weights):
    depth, width = weights[0].shape
    count = len(weights)
    return pl.pallas_call(
        stage_body,
        in_specs=[pl.BlockSpec(memory_space=pl.ANY)] * count,
        out_specs=pl.BlockSpec(memory_space=pltpu.VMEM),
        out_shape=jax.ShapeDtypeStruct((count * depth, width), jnp.bfloat16),
        scratch_shapes=[pltpu.SemaphoreType.DMA((count,))],
        compiler_params=pltpu.CompilerParams(vmem_limit_bytes=4 << 20),
        cost_estimate=pl.CostEstimate(flops=0, bytes_accessed=4 * count * depth * width, transcendentals=0),
        name="stage",
    )(*weights)


def arrange(meta, parts, left):
    sides = len(parts) // 4
    n_rows, lanes = parts[0].shape
    depth = lanes // 4
    z, tensor, y_low = meta[0], meta[1], meta[2]
    for rel, shift in enumerate((0, 1, 3, 2)):
        for zz in range(2):
            slot = (z - (2 * ((tensor + 4 - shift) % 4) + zz) + 8) % 8
            for side in range(sides):
                ref = parts[sides * rel + side]
                rows = slice(side * n_rows, (side + 1) * n_rows)

                @pl.when(y_low == 0)
                def _(slot=slot, ref=ref, rows=rows, zz=zz):
                    left[slot, rows] = ref[:, 2 * zz * depth : (2 * zz + 2) * depth]

                @pl.when(y_low != 0)
                def _(slot=slot, ref=ref, rows=rows, zz=zz):
                    left[slot, rows, 0:depth] = ref[:, (2 * zz + 1) * depth : (2 * zz + 2) * depth]
                    left[slot, rows, depth : 2 * depth] = ref[:, 2 * zz * depth : (2 * zz + 1) * depth]


def multiply(left, staged, own, other, begin):
    n_rows, width = own.shape

    def chunk(c, carry):
        at = pl.multiple_of(c * CHUNK, CHUNK)
        whole = jnp.concatenate([left[k] for k in range(8)], axis=1)
        total = jnp.dot(whole, staged[:, pl.ds(begin + at, CHUNK)], preferred_element_type=jnp.float32)
        own[:, pl.ds(at, CHUNK)] = total[:n_rows]
        other[:, pl.ds(at, CHUNK)] = total[n_rows:].astype(jnp.bfloat16)
        return carry

    lax.fori_loop(0, width // CHUNK, chunk, 0)


def first_body(meta, *refs):
    parts, (staged, own, other, left) = refs[:-4], refs[-4:]
    arrange(meta, parts, left)
    multiply(left, staged, own, other, 0)


def later_body(left, staged, own, other, begin):
    multiply(left, staged, own, other, begin)


def project(meta, parts, staged, width, begin=0, left=None):
    rows = parts[0].shape[0] * len(parts) // 8
    lanes = parts[0].shape[1]
    depth = staged.shape[0]
    vmem = pl.BlockSpec(memory_space=pltpu.VMEM)
    result = [jax.ShapeDtypeStruct((rows, width), kind) for kind in (jnp.float32, jnp.bfloat16)]
    options = dict(
        compiler_params=pltpu.CompilerParams(vmem_limit_bytes=12 << 20),
        cost_estimate=pl.CostEstimate(
            flops=4 * rows * depth * width, bytes_accessed=2 * depth * width, transcendentals=0
        ),
        name="project",
    )
    if left is None:
        return pl.pallas_call(
            first_body,
            in_specs=[pl.BlockSpec(memory_space=pltpu.SMEM)] + [vmem] * (len(parts) + 1),
            out_specs=[vmem] * 3,
            out_shape=[*result, jax.ShapeDtypeStruct((8, 2 * rows, lanes // 2), jnp.bfloat16)],
            **options,
        )(meta, *parts, staged)
    return pl.pallas_call(
        functools.partial(later_body, begin=begin),
        in_specs=[vmem] * 2,
        out_specs=[vmem] * 2,
        out_shape=result,
        **options,
    )(left, staged)


def per_device(resid, streams, filt, q_gain, k_gain, out_weight, contig_lengths):
    resid_own = resid[0]
    streams_own = jnp.transpose(streams[0], (0, 2, 1, 3))
    rows = resid_own.shape[1]
    section = lax.axis_index("pipe")
    seq = lax.axis_index("seq")
    tensor = lax.axis_index("tensor")
    n_seq = lax.axis_size("seq")
    n_tensor = lax.axis_size("tensor")
    n_z = n_seq // 4
    core = seq % 2
    y_low = (seq // 2) % 2
    both = ("pipe", "seq")

    def along_y(value, step):
        pairs = []
        for y in range(4):
            to = (y + step) % 4
            for z in range(n_z):
                for c in range(2):
                    pairs.append(((y // 2) * n_seq + z * 4 + (y % 2) * 2 + c, (to // 2) * n_seq + z * 4 + (to % 2) * 2 + c))
        return lax.ppermute(value, both, pairs)

    def along_z(value, step):
        return lax.ppermute(value, "seq", [(s, (s + 4 * step) % n_seq) for s in range(n_seq)])

    def along_tensor(value, step):
        return lax.ppermute(value, "tensor", [(t, (t + step) % n_tensor) for t in range(n_tensor)])

    partner = [(s, s ^ 1) for s in range(n_seq)]
    tail = tail_of(streams_own)
    prev = lax.ppermute(tail, "seq", [(s, s + 1) for s in range(n_seq - 1)])
    output, attend_1 = hyena(streams_own, resid_own, prev, filt, 1)
    arrived = lax.ppermute(attend_1, "pipe", [(0, 1)])
    output, attend_0 = hyena(streams_own, resid_own, prev, filt, 0, output)

    right, left = [out_weight], [out_weight]
    across = {0: along_y(out_weight, 1)}
    for k in range(1, 5):
        right.append(along_z(right[-1], 1))
        across[k] = along_y(right[k], 1 if k < 4 else -1)
        if k < 4:
            left.append(along_z(left[-1], -1))
            across[8 - k] = along_y(left[k], -1)
    same = right + [left[k] for k in (3, 2, 1)]
    weights = []
    for k in range(8):
        weights += [same[k], across[k]]

    contig_ends = jnp.cumsum(contig_lengths, axis=1)[section]
    start = seq * rows
    query_pos = start + jnp.arange(rows, dtype=jnp.int32)
    low = jnp.max(jnp.where(contig_ends[None, :] <= query_pos[:, None], contig_ends[None, :], 0), axis=1)
    first_low = jnp.max(jnp.where(contig_ends <= start, contig_ends, 0))
    count = 1 + (start - first_low + rows - 1) // rows
    slots = jnp.arange(8, dtype=jnp.int32)
    split = rows * 7 // 16
    meta = jnp.where(slots < 5, start - rows * slots, jnp.where(slots == 5, count, core))
    low = jnp.broadcast_to(low[:, None], (rows, HD)).astype(jnp.int32)
    gain = q_gain[None, :] * (1.0 / HD)
    attend_0, meta, low, gain = lax.optimization_barrier((attend_0, meta, low, gain))
    own = jnp.where(section == 0, attend_0, arrived)
    behind = lax.ppermute(own, "seq", [(s, s + 4) for s in range(n_seq - 4)])
    mid = lax.ppermute(jnp.where(y_low == 0, own, behind), "seq", [(s, s ^ 2) for s in range(n_seq)])
    beside = lax.ppermute(jnp.where(core == 0, own, behind), "seq", partner)
    beside_2 = lax.ppermute(mid, "seq", partner)
    pieces = (own, behind, mid, beside, beside_2)

    keep, give, pack = attention(
        meta, pieces, low, gain, k_gain[None, :], rows - split
    )

    got = lax.ppermute(give, "seq", partner)
    keep_1, keep_3 = along_tensor(keep, 1), along_tensor(keep, -1)
    got_1, got_3 = along_tensor(got, 1), along_tensor(got, -1)
    pack = lax.dynamic_update_slice(pack, got[split:], (rows - split, 0))
    below = lax.ppermute(pack, "pipe", [(0, 1)])
    keep_2, got_2 = along_tensor(keep_1, 1), along_tensor(got_3, -1)
    parts = [keep, got, keep_1, got_1, keep_3, got_3, keep_2, got_2]
    below_parts = [below] + [along_tensor(below, step) for step in (1, -1, 2)]
    place = jnp.where(slots == 0, seq // 4, jnp.where(slots == 1, tensor, y_low))

    def put(output, batch, row, col, value):
        at = (batch, row, col)
        old = lax.dynamic_slice(output, at, (1,) + value.shape)
        return lax.dynamic_update_slice(output, jnp.where(section == 0, old, value[None]), at)

    staged = stage(weights)
    width = staged.shape[1] // HALVES
    returned, lhs = [], None
    for half in range(HALVES):
        own, other, *rest = project(place, parts, staged, width, half * width, lhs)
        lhs = rest[0] if rest else lhs
        other = lax.ppermute(other, "seq", partner)
        part = (own + other).astype(jnp.bfloat16)
        returned.append(lax.ppermute(part[:split], "pipe", [(0, 1)]))
        output = put(output, 1, 0, half * width, part)
    own, other, _ = project(place, below_parts, staged, staged.shape[1])
    other = lax.ppermute(other, "seq", partner)
    output = put(output, 0, split, 0, (own + other).astype(jnp.bfloat16))
    for half in range(HALVES):
        output = put(output, 0, 0, half * width, returned[half])
    return output[None]


def solution(mesh):
    placed = (
        P("pipe", None, "seq", "tensor"),
        P("pipe", None, "seq", None, "tensor"),
        P(None, "tensor"),
        P("tensor"),
        P("tensor"),
        P("seq", "tensor"),
        P(),
    )
    return jax.shard_map(
        per_device,
        mesh=mesh,
        in_specs=placed,
        out_specs=P("pipe", None, "seq", "tensor"),
        check_vma=False,
    )
```
